128 devices in a mesh: slide: 32 (over z, x, core), ctx: 4 (over y).
Axes of the slice: x: 4, y: 4, z: 4, core: 2. Of those that a mesh axis runs over, the one named last changes fastest.
Arguments:
- feature_maps: bfloat16 [4096, 16, 16, 384], P(('slide', 'ctx')), may hold values from -6 to 6
- down_weight: bfloat16 [1536, 768], replicated, may hold values from -0.15625 to 0.15625
- conv_taps: bfloat16 [49, 768], replicated, may hold values from -0.875 to 0.875
- mlp_in: bfloat16 [768, 3072], replicated, may hold values from -0.21875 to 0.21875
- mlp_out: bfloat16 [3072, 768], replicated, may hold values from -0.109375 to 0.109375
- layer_scale: float32 [768], replicated, may hold values from 0.2 to 1
- qkv_weight: bfloat16 [1, 768, 2304], replicated, may hold values from -4.690971 to 4.690971
- out_weight: bfloat16 [1, 768, 768], replicated, may hold values from -0.21875 to 0.21875
- tile_slide: int32 [4096], P(('slide', 'ctx')), may hold values from 0 to 31, as said below
- tile_pos: int32 [4096], P(('slide', 'ctx')), may hold values from 0 to 767, as said below
- slide_len: int32 [32], replicated, may hold values from 1 to 768, as said below
Outputs:
- slide_tokens: bfloat16 [24576, 768], P(('slide', 'ctx'))
The draws below stay inside these ranges and needn't reach their ends.
Inputs may be any that keep to these rules, and one draw needn't show every extreme that they name: `tile_slide`: the tiles of slide s lie at positions 0 to slide_len[s] - 1 of it, exactly one tile at each. `tile_pos`: among the tiles of one device at most 2 lie in the same block of 192 positions of one slide, and some device has exactly 2 in some block. `slide_len`: the lengths sum to 4096; some slide has exactly 768 tiles.
All inputs are finite; a program needn't handle non-finite values.
Results may differ from the reference program's by a relative error of at most 0.015.
Values may be sent and summed in bfloat16 or wider, within the bound.
A program may use at most 128 MiB of HBM per device.

```python
import math
import jax
import jax.numpy as jnp
from jax import lax

C_IN = 384
D = 768
MLP_DIM = 3072
HEADS = 12
HEAD_DIM = 64
MAP = 16
KS = 7
LAYERS = 1
TILES_DEV = 32
SLIDES = 32
SEQ = 768
TILES = 4096
SLOTS = 24576


def tile_layout(key):
    layout_key = jax.random.fold_in(key, 7)
    lead_key, pair_key, order_key, source_key, local_key = jax.random.split(layout_key, 5)
    mean_len = TILES // SLIDES
    rest_sum = 8 * mean_len - SEQ
    part_sum = rest_sum // 4
    lead_cuts = jax.random.randint(lead_key, (3,), 1, part_sum, dtype=jnp.int32)
    leading = jnp.concatenate([jnp.full((1,), SEQ, jnp.int32), lead_cuts, part_sum - lead_cuts, jnp.full((1,), rest_sum - 3 * part_sum, jnp.int32)]).astype(jnp.int32)
    paired = jax.random.randint(pair_key, ((SLIDES - 8) // 2,), 1, 2 * mean_len, dtype=jnp.int32)
    lengths = jnp.concatenate([leading, paired, 2 * mean_len - paired]).astype(jnp.int32)
    lengths = lengths[jax.random.permutation(order_key, SLIDES)]
    starts = (jnp.cumsum(lengths) - lengths).astype(jnp.int32)
    flat_index = jnp.arange(TILES, dtype=jnp.int32)
    slide_of = jnp.sum((starts[None, :] <= flat_index[:, None]).astype(jnp.int32), axis=1) - 1
    place_of = flat_index - starts[slide_of]
    device_total = TILES // TILES_DEV
    source_order = jax.random.permutation(source_key, device_total).astype(jnp.int32)
    local_order = jax.random.permutation(local_key, TILES_DEV).astype(jnp.int32)
    landing = source_order[flat_index % device_total] * TILES_DEV + local_order[flat_index // device_total]
    slide_list = jnp.zeros((TILES,), jnp.int32).at[landing].set(slide_of.astype(jnp.int32))
    place_list = jnp.zeros((TILES,), jnp.int32).at[landing].set(place_of.astype(jnp.int32))
    return (slide_list, place_list, lengths)


def draw_tile_slide(key, part):
    return tile_layout(key)[0]


def draw_tile_pos(key, part):
    return tile_layout(key)[1]


def draw_slide_len(key, part):
    return tile_layout(key)[2]


def draw_qkv_weight(key, part):
    base_key = jax.random.fold_in(jax.random.fold_in(key, 11), 0)
    matrix = jax.random.truncated_normal(base_key, -4.0, 4.0, (LAYERS, D, 3 * D), jnp.float32) * D ** (-0.5)
    return matrix.astype(jnp.bfloat16)


def block_levels(rng, extent, cuts, smallest, largest):
    level = 1.0
    for position, blocks in cuts:
        heights = jax.random.uniform(jax.random.fold_in(jax.random.fold_in(rng, 6), position), (blocks,), jnp.float32, smallest / len(cuts), largest / len(cuts))
        level = level * jnp.repeat(jnp.exp(heights), extent[position] // blocks).reshape((-1,) + (1,) * (len(extent) - 1 - position))
    return level


def centred(rng, extent, scale, limit, cuts=(), held_as=jnp.bfloat16):
    values = jax.random.normal(rng, extent, jnp.float32) * scale
    if len(cuts) > 0:
        values = block_levels(rng, extent, cuts, -0.22, 0.18) * values
    return jnp.clip(values, min=-limit, max=limit).astype(held_as)


def setup_inputs(seed: int = 0) -> dict:
    arg_keys = jax.random.split(jax.random.key(seed), 12)
    feature_maps = centred(arg_keys[0], (TILES, MAP, MAP, C_IN), 1.0, 6.0, ((0, 128),))
    down_weight = centred(arg_keys[1], (4 * C_IN, D), (4 * C_IN) ** -0.5, 0.15625)
    conv_taps = centred(arg_keys[2], (KS * KS, D), (KS * KS) ** -0.5, 0.875)
    mlp_in = centred(arg_keys[3], (D, MLP_DIM), D ** -0.5, 0.21875)
    mlp_out = centred(arg_keys[4], (MLP_DIM, D), MLP_DIM ** -0.5, 0.109375)
    layer_scale = jnp.clip(jnp.exp(jax.random.uniform(arg_keys[5], (D,), jnp.float32, math.log(0.2), math.log(1.0))), 0.2, 1.0)
    qkv_weight = draw_qkv_weight(jax.random.fold_in(arg_keys[11], 71), 0)
    out_weight = centred(arg_keys[7], (LAYERS, D, D), D ** -0.5, 0.21875)
    tile_slide = draw_tile_slide(jax.random.fold_in(arg_keys[11], 71), 0)
    tile_pos = draw_tile_pos(jax.random.fold_in(arg_keys[11], 71), 0)
    slide_len = draw_slide_len(jax.random.fold_in(arg_keys[11], 71), 0)
    return dict(feature_maps=feature_maps, down_weight=down_weight, conv_taps=conv_taps, mlp_in=mlp_in, mlp_out=mlp_out, layer_scale=layer_scale, qkv_weight=qkv_weight, out_weight=out_weight, tile_slide=tile_slide, tile_pos=tile_pos, slide_len=slide_len)


NORM_EPS = 1e-06
FAR_NEGATIVE = -1e+30

def layer_norm(values):
    center = values - lax.optimization_barrier(jnp.mean(values, axis=-1, keepdims=True))
    spread = lax.optimization_barrier(jnp.mean(center * center, axis=-1, keepdims=True))
    return center * lax.rsqrt(spread + NORM_EPS)

def encode_tiles(tile_maps, down_weight, conv_taps, mlp_in, mlp_out, layer_scale):
    tile_count = tile_maps.shape[0]
    half_side = MAP // 2
    normed = layer_norm(tile_maps.astype(jnp.float32)).astype(jnp.bfloat16)
    patches = normed.reshape(tile_count, half_side, 2, half_side, 2, C_IN).transpose(0, 1, 3, 2, 4, 5)
    patches = patches.reshape(tile_count * half_side * half_side, 4 * C_IN)
    reduced = jnp.dot(patches, down_weight, preferred_element_type=jnp.float32).astype(jnp.bfloat16)
    widened = reduced.reshape(tile_count, half_side, half_side, D).astype(jnp.float32)
    tap_values = conv_taps.astype(jnp.float32)
    pad_reach = KS // 2
    padded = jnp.pad(widened, ((0, 0), (pad_reach, pad_reach), (pad_reach, pad_reach), (0, 0)))
    spatial = jnp.zeros_like(widened)
    for row_off in range(KS):
        for col_off in range(KS):
            spatial = spatial + padded[:, row_off:row_off + half_side, col_off:col_off + half_side, :] * tap_values[row_off * KS + col_off]
    spatial_normed = layer_norm(spatial).astype(jnp.bfloat16).reshape(tile_count * half_side * half_side, D)
    expanded = jax.nn.gelu(jnp.dot(spatial_normed, mlp_in, preferred_element_type=jnp.float32), approximate=False).astype(jnp.bfloat16)
    branch = jnp.dot(expanded, mlp_out, preferred_element_type=jnp.float32)
    blocked = widened + (layer_scale * branch).reshape(tile_count, half_side, half_side, D)
    pooled = lax.optimization_barrier(jnp.mean(blocked, axis=(1, 2)))
    return layer_norm(pooled).astype(jnp.bfloat16)

def attend_slide(slot_rows, length, qkv_weight, out_weight):
    valid = jnp.arange(SEQ, dtype=jnp.int32) < length
    stream = slot_rows.astype(jnp.float32)
    for layer_idx in range(LAYERS):
        lnorm = layer_norm(stream).astype(jnp.bfloat16)
        packed = jnp.dot(lnorm, qkv_weight[layer_idx], preferred_element_type=jnp.float32).astype(jnp.bfloat16)
        queries = packed[:, :D].reshape(SEQ, HEADS, HEAD_DIM).astype(jnp.float32)
        keys_all = packed[:, D:2 * D].reshape(SEQ, HEADS, HEAD_DIM).astype(jnp.float32)
        values_all = packed[:, 2 * D:].reshape(SEQ, HEADS, HEAD_DIM).astype(jnp.float32)
        scores = jnp.einsum('qhe,khe->hqk', queries, keys_all) * HEAD_DIM ** (-0.5)
        scores = jnp.where(valid[None, None, :], scores, FAR_NEGATIVE)
        peak = lax.optimization_barrier(jnp.max(scores, axis=-1, keepdims=True))
        weights = jnp.where(valid[None, None, :], jnp.exp(scores - peak), 0.0)
        denom = lax.optimization_barrier(jnp.sum(weights, axis=-1))
        weights_bf = lax.optimization_barrier(weights.astype(jnp.bfloat16)).astype(jnp.float32)
        attended = jnp.einsum('hqk,khe->qhe', weights_bf, values_all) / jnp.transpose(denom)[:, :, None]
        attended = attended.reshape(SEQ, D).astype(jnp.bfloat16)
        stream = stream + jnp.dot(attended, out_weight[layer_idx], preferred_element_type=jnp.float32)
    return jnp.where(valid[:, None], stream, 0.0).astype(jnp.bfloat16)

def reference(feature_maps, down_weight, conv_taps, mlp_in, mlp_out, layer_scale, qkv_weight, out_weight, tile_slide, tile_pos, slide_len):
    tile_blocks = feature_maps.reshape(TILES // TILES_DEV, TILES_DEV, MAP, MAP, C_IN)
    embeds = lax.map(lambda tile_maps: encode_tiles(tile_maps, down_weight, conv_taps, mlp_in, mlp_out, layer_scale), tile_blocks)
    embeds = embeds.reshape(TILES, D)
    target = (tile_slide * SEQ + tile_pos).astype(jnp.int32)
    slot_table = jnp.zeros((SLOTS, D), jnp.bfloat16).at[target].set(embeds)
    outputs = lax.map(lambda pair: attend_slide(pair[0], pair[1], qkv_weight, out_weight), (slot_table.reshape(SLIDES, SEQ, D), slide_len))
    return outputs.reshape(SLOTS, D)
```

```python
import jax
import jax.numpy as jnp
from jax import lax
from jax.experimental import pallas as pl
from jax.experimental.pallas import tpu as pltpu

NORM_EPS = 1e-06
GROUP = 8
HALF = 8
KS = 7
C_IN = 384
D = 768
LB = D // 128
MLP = 3072
HC = 512
PITCH = 257
UA = 4
UD = 4
INV_SQRT2 = 0.7071067811865476

def double_gelu(v):
    return v + v * lax.erf(v * INV_SQRT2)

def encode_kernel(x_ref, down_ref, taps_ref, w1_ref, w2_ref, ls_ref, out_ref,
                  s_ref, l_ref, r_ref, sp_ref, sn_ref, tap_ref, ph_ref, pr_ref):
    g = pl.program_id(0)

    @pl.when(g == 0)
    def _():
        t = taps_ref[...].astype(jnp.float32)
        for k in range(KS * KS):
            for l in range(LB):
                tap_ref[l, k] = jnp.broadcast_to(t[k:k + 1, l * 128:(l + 1) * 128], (8, 128))

    def norm_rows(n, _):
        t = n // 4
        y = (n % 4) * 4
        x = x_ref[t, pl.ds(y, 4)].reshape(64, C_IN).astype(jnp.float32)
        c = x - jnp.mean(x, axis=-1, keepdims=True)
        v = jnp.mean(c * c, axis=-1, keepdims=True)
        o = c * lax.rsqrt(v + NORM_EPS)
        base = t * PITCH + y * 16
        for l in range(3):
            s_ref[l, pl.ds(base, 64), :] = o[:, l * 128:(l + 1) * 128]
        return 0
    lax.fori_loop(0, GROUP * 4, norm_rows, 0, unroll=UA)

    def patch_rows(n, _):
        i = n // 4
        jp = (n % 4) * 2
        row = pl.multiple_of((i * HALF + jp) * GROUP, 16)
        for dy in range(2):
            for dx in range(2):
                for l in range(3):
                    pos = (2 * i + dy) * 16 + 2 * jp + dx
                    a = s_ref[l, pl.ds(pos, GROUP, stride=PITCH), :]
                    b = s_ref[l, pl.ds(pos + 2, GROUP, stride=PITCH), :]
                    col = (dy * 2 + dx) * C_IN + l * 128
                    l_ref[pl.ds(row, 16), col:col + 128] = jnp.concatenate([a, b], axis=0).astype(jnp.bfloat16)
        return 0
    lax.fori_loop(0, HALF * HALF // 2, patch_rows, 0, unroll=2)

    for n in range(3):
        red = jnp.dot(l_ref[...], down_ref[:, n * 256:(n + 1) * 256], preferred_element_type=jnp.float32)
        red = red.astype(jnp.bfloat16).astype(jnp.float32)
        for h in range(2):
            r_ref[n * 2 + h] = red[:, h * 128:(h + 1) * 128].reshape(64, GROUP, 128)

    def conv_lane(l, _):
        psum = jnp.zeros((GROUP, 128), jnp.float32)
        for i in range(HALF):
            acc = [None] * HALF
            for a in range(KS):
                ii = i + a - 3
                if not 0 <= ii < HALF:
                    continue
                xs = [r_ref[l, ii * HALF + j] for j in range(HALF)]
                for b in range(KS):
                    w = tap_ref[l, a * KS + b]
                    for j in range(HALF):
                        jj = j + b - 3
                        if 0 <= jj < HALF:
                            term = xs[jj] * w
                            acc[j] = term if acc[j] is None else acc[j] + term
                if ii == i:
                    for j in range(HALF):
                        psum = psum + xs[j]
            for j in range(HALF):
                sp_ref[l, i * HALF + j] = acc[j]
        pr_ref[l, pl.ds(pl.multiple_of(g * GROUP, GROUP), GROUP), :] = psum
        return 0
    lax.fori_loop(0, LB, conv_lane, 0)

    def norm_spatial(n, _):
        rows = [sp_ref[l, pl.ds(n * 8, 8)].reshape(64, 128) for l in range(LB)]
        tot = rows[0]
        for r in rows[1:]:
            tot = tot + r
        mean = jnp.sum(tot, axis=-1, keepdims=True) * (1.0 / D)
        cs = [r - mean for r in rows]
        sq = cs[0] * cs[0]
        for c in cs[1:]:
            sq = sq + c * c
        var = jnp.sum(sq, axis=-1, keepdims=True) * (1.0 / D)
        inv = lax.rsqrt(var + NORM_EPS)
        for l in range(LB):
            sn_ref[pl.ds(pl.multiple_of(n * 64, 64), 64), l * 128:(l + 1) * 128] = (cs[l] * inv).astype(jnp.bfloat16)
        return 0
    lax.fori_loop(0, 8, norm_spatial, 0, unroll=UD)

    for c in range(MLP // HC):
        h = jnp.dot(sn_ref[...], w1_ref[:, c * HC:(c + 1) * HC], preferred_element_type=jnp.float32)
        h = double_gelu(h)
        ph_ref[pl.ds(pl.multiple_of(g * GROUP, GROUP), GROUP), c * HC:(c + 1) * HC] = jnp.sum(
            h.reshape(64, GROUP, HC), axis=0)

    @pl.when(g == pl.num_programs(0) - 1)
    def _():
        p = ph_ref[...]
        hi = p.astype(jnp.bfloat16)
        lo = (p - hi.astype(jnp.float32)).astype(jnp.bfloat16)
        br = jnp.dot(jnp.concatenate([hi, lo], axis=0), w2_ref[...], preferred_element_type=jnp.float32)
        nt = p.shape[0]
        br = br[:nt] + br[nt:]
        pr = jnp.concatenate([pr_ref[l] for l in range(LB)], axis=-1)
        pooled = (pr + ls_ref[...] * (0.5 * br)) * (1.0 / 64)
        c = pooled - jnp.mean(pooled, axis=-1, keepdims=True)
        v = jnp.mean(c * c, axis=-1, keepdims=True)
        out_ref[...] = (c * lax.rsqrt(v + NORM_EPS)).astype(jnp.bfloat16)

def encode_tiles(x, down, taps, w1, w2, ls):
    nt = x.shape[0]
    one = pl.Buffered(1)
    full = lambda s: pl.BlockSpec(s, lambda g: (0,) * len(s), pipeline_mode=one)
    return pl.pallas_call(
        encode_kernel,
        out_shape=jax.ShapeDtypeStruct((nt, D), jnp.bfloat16),
        grid=(nt // GROUP,),
        in_specs=[
            pl.BlockSpec((GROUP, 16, 16, C_IN), lambda g: (g, 0, 0, 0)),
            full((4 * C_IN, D)), full((KS * KS, D)), full((D, MLP)), full((MLP, D)), full((1, D)),
        ],
        out_specs=pl.BlockSpec((nt, D), lambda g: (0, 0)),
        scratch_shapes=[
            pltpu.VMEM((3, GROUP * PITCH, 128), jnp.float32),
            pltpu.VMEM((64 * GROUP, 4 * C_IN), jnp.bfloat16),
            pltpu.VMEM((LB, 64, GROUP, 128), jnp.float32),
            pltpu.VMEM((LB, 64, GROUP, 128), jnp.float32),
            pltpu.VMEM((64 * GROUP, D), jnp.bfloat16),
            pltpu.VMEM((LB, KS * KS, 8, 128), jnp.float32),
            pltpu.VMEM((nt, MLP), jnp.float32),
            pltpu.VMEM((LB, nt, 128), jnp.float32),
        ],
        compiler_params=pltpu.CompilerParams(vmem_limit_bytes=56 << 20),
        name="encode",
    )(x, down, taps, w1, w2, ls.reshape(1, D))


from jax.sharding import PartitionSpec as P

HEADS = 12
HEAD_DIM = 64
SEQ_DEV = 192
FAR_NEGATIVE = -1e30


def layer_norm(values):
    center = values - jnp.mean(values, axis=-1, keepdims=True)
    spread = jnp.mean(center * center, axis=-1, keepdims=True)
    return center * lax.rsqrt(spread + NORM_EPS)


def shards(feature_maps, down_weight, conv_taps, mlp_in, mlp_out, layer_scale, qkv_weight, out_weight,
           tile_slide, tile_pos, slide_len):
    ctx_count = lax.axis_size("ctx")
    device_count = lax.axis_size("slide") * ctx_count
    capacity = (SEQ_DEV + device_count - 1) // device_count
    tiles_here = feature_maps.shape[0]
    embeds = encode_tiles(feature_maps, down_weight, conv_taps, mlp_in, mlp_out, layer_scale)
    owner_index = tile_slide * ctx_count + tile_pos // SEQ_DEV
    tile_order = jnp.arange(tiles_here, dtype=jnp.int32)
    earlier = (owner_index[None, :] == owner_index[:, None]) & (tile_order[None, :] < tile_order[:, None])
    tile_rank = jnp.sum(earlier.astype(jnp.int32), axis=1)
    target_row = owner_index * capacity + tile_rank
    placing = jnp.arange(device_count * capacity, dtype=jnp.int32)[:, None] == target_row[None, :]
    slot_code = (tile_pos % SEQ_DEV + 1).astype(jnp.bfloat16)
    coded = jnp.concatenate([embeds, jnp.broadcast_to(slot_code[:, None], (tiles_here, 128))], axis=1)
    outgoing = jnp.dot(placing.astype(jnp.bfloat16), coded, preferred_element_type=jnp.float32).astype(jnp.bfloat16)
    arrived = lax.all_to_all(outgoing, ("slide", "ctx"), split_axis=0, concat_axis=0, tiled=True)
    arrived_slot = arrived[:, D].astype(jnp.int32) - 1
    position = jnp.arange(SEQ_DEV, dtype=jnp.int32)
    picking = (position[:, None] == arrived_slot[None, :]).astype(jnp.bfloat16)
    slot_rows = jnp.dot(picking, arrived[:, :D], preferred_element_type=jnp.float32).astype(jnp.bfloat16)
    all_rows = lax.all_gather(slot_rows, "ctx", axis=0, tiled=True)
    length = slide_len[lax.axis_index("slide")]
    query_pos = lax.axis_index("ctx") * SEQ_DEV + position
    stream = slot_rows.astype(jnp.float32)
    lnorm = layer_norm(stream).astype(jnp.bfloat16)
    lnorm_all = layer_norm(all_rows.astype(jnp.float32)).astype(jnp.bfloat16)
    queries = jnp.dot(lnorm, qkv_weight[0, :, :D], preferred_element_type=jnp.float32).astype(jnp.bfloat16)
    queries = queries.reshape(SEQ_DEV, HEADS, HEAD_DIM)
    key_rows = jnp.dot(lnorm_all, qkv_weight[0, :, D:], preferred_element_type=jnp.float32).astype(jnp.bfloat16)
    row_count = key_rows.shape[0]
    keys_part = key_rows[:, :D].reshape(row_count, HEADS, HEAD_DIM)
    values_part = key_rows[:, D:].reshape(row_count, HEADS, HEAD_DIM)
    scores = jnp.einsum("qhe,khe->hqk", queries, keys_part, preferred_element_type=jnp.float32) * HEAD_DIM ** (-0.5)
    included = jnp.arange(row_count, dtype=jnp.int32) < length
    scores = jnp.where(included[None, None, :], scores, FAR_NEGATIVE)
    peak = jnp.max(scores, axis=-1)
    weights = jnp.where(included[None, None, :], jnp.exp(scores - peak[:, :, None]), 0.0)
    denom_sum = jnp.sum(weights, axis=-1)
    accum = jnp.einsum("hqk,khe->hqe", weights.astype(jnp.bfloat16), values_part, preferred_element_type=jnp.float32)
    attended = (accum / denom_sum[:, :, None]).transpose(1, 0, 2).reshape(SEQ_DEV, D).astype(jnp.bfloat16)
    stream = stream + jnp.dot(attended, out_weight[0], preferred_element_type=jnp.float32)
    return jnp.where((query_pos < length)[:, None], stream, 0.0).astype(jnp.bfloat16)


def solution(mesh):
    whole = P(("slide", "ctx"))
    return jax.shard_map(
        shards,
        mesh=mesh,
        in_specs=(whole, P(), P(), P(), P(), P(), P(), P(), whole, whole, P()),
        out_specs=whole,
        check_vma=False,
    )
```

```python
import jax
import jax.numpy as jnp
from jax import lax
from jax.experimental import pallas as pl
from jax.experimental.pallas import tpu as pltpu

NORM_EPS = 1e-06
GROUP = 8
HALF = 8
KS = 7
C_IN = 384
D = 768
LB = D // 128
MLP = 3072
HC = 512
PITCH = 257
UA = 4
UD = 4
INV_SQRT2 = 0.7071067811865476

def double_gelu(v):
    return v + v * lax.erf(v * INV_SQRT2)

def encode_kernel(x_ref, down_ref, taps_ref, w1_ref, w2_ref, ls_ref, out_ref,
                  s_ref, l_ref, r_ref, sp_ref, sn_ref, tap_ref, ph_ref, pr_ref):
    g = pl.program_id(0)

    @pl.when(g == 0)
    def _():
        t = taps_ref[...].astype(jnp.float32)
        for k in range(KS * KS):
            for l in range(LB):
                tap_ref[l, k] = jnp.broadcast_to(t[k:k + 1, l * 128:(l + 1) * 128], (8, 128))

    def norm_rows(n, _):
        t = n // 4
        y = (n % 4) * 4
        x = x_ref[t, pl.ds(y, 4)].reshape(64, C_IN).astype(jnp.float32)
        c = x - jnp.mean(x, axis=-1, keepdims=True)
        v = jnp.mean(c * c, axis=-1, keepdims=True)
        o = c * lax.rsqrt(v + NORM_EPS)
        base = t * PITCH + y * 16
        for l in range(3):
            s_ref[l, pl.ds(base, 64), :] = o[:, l * 128:(l + 1) * 128]
        return 0
    lax.fori_loop(0, GROUP * 4, norm_rows, 0, unroll=UA)

    def patch_rows(n, _):
        i = n // 4
        jp = (n % 4) * 2
        row = pl.multiple_of((i * HALF + jp) * GROUP, 16)
        for dy in range(2):
            for dx in range(2):
                for l in range(3):
                    pos = (2 * i + dy) * 16 + 2 * jp + dx
                    a = s_ref[l, pl.ds(pos, GROUP, stride=PITCH), :]
                    b = s_ref[l, pl.ds(pos + 2, GROUP, stride=PITCH), :]
                    col = (dy * 2 + dx) * C_IN + l * 128
                    l_ref[pl.ds(row, 16), col:col + 128] = jnp.concatenate([a, b], axis=0).astype(jnp.bfloat16)
        return 0
    lax.fori_loop(0, HALF * HALF // 2, patch_rows, 0, unroll=2)

    for n in range(3):
        red = jnp.dot(l_ref[...], down_ref[:, n * 256:(n + 1) * 256], preferred_element_type=jnp.float32)
        red = red.astype(jnp.bfloat16).astype(jnp.float32)
        for h in range(2):
            r_ref[n * 2 + h] = red[:, h * 128:(h + 1) * 128].reshape(64, GROUP, 128)

    def conv_lane(l, _):
        psum = jnp.zeros((GROUP, 128), jnp.float32)
        for i in range(HALF):
            acc = [None] * HALF
            for a in range(KS):
                ii = i + a - 3
                if not 0 <= ii < HALF:
                    continue
                xs = [r_ref[l, ii * HALF + j] for j in range(HALF)]
                for b in range(KS):
                    w = tap_ref[l, a * KS + b]
                    for j in range(HALF):
                        jj = j + b - 3
                        if 0 <= jj < HALF:
                            term = xs[jj] * w
                            acc[j] = term if acc[j] is None else acc[j] + term
                if ii == i:
                    for j in range(HALF):
                        psum = psum + xs[j]
            for j in range(HALF):
                sp_ref[l, i * HALF + j] = acc[j]
        pr_ref[l, pl.ds(pl.multiple_of(g * GROUP, GROUP), GROUP), :] = psum
        return 0
    lax.fori_loop(0, LB, conv_lane, 0)

    def norm_spatial(n, _):
        rows = [sp_ref[l, pl.ds(n * 8, 8)].reshape(64, 128) for l in range(LB)]
        tot = rows[0]
        for r in rows[1:]:
            tot = tot + r
        mean = jnp.sum(tot, axis=-1, keepdims=True) * (1.0 / D)
        cs = [r - mean for r in rows]
        sq = cs[0] * cs[0]
        for c in cs[1:]:
            sq = sq + c * c
        var = jnp.sum(sq, axis=-1, keepdims=True) * (1.0 / D)
        inv = lax.rsqrt(var + NORM_EPS)
        for l in range(LB):
            sn_ref[pl.ds(pl.multiple_of(n * 64, 64), 64), l * 128:(l + 1) * 128] = (cs[l] * inv).astype(jnp.bfloat16)
        return 0
    lax.fori_loop(0, 8, norm_spatial, 0, unroll=UD)

    for c in range(MLP // HC):
        h = jnp.dot(sn_ref[...], w1_ref[:, c * HC:(c + 1) * HC], preferred_element_type=jnp.float32)
        h = double_gelu(h)
        ph_ref[pl.ds(pl.multiple_of(g * GROUP, GROUP), GROUP), c * HC:(c + 1) * HC] = jnp.sum(
            h.reshape(64, GROUP, HC), axis=0)

    @pl.when(g == pl.num_programs(0) - 1)
    def _():
        p = ph_ref[...]
        hi = p.astype(jnp.bfloat16)
        lo = (p - hi.astype(jnp.float32)).astype(jnp.bfloat16)
        br = jnp.dot(jnp.concatenate([hi, lo], axis=0), w2_ref[...], preferred_element_type=jnp.float32)
        nt = p.shape[0]
        br = br[:nt] + br[nt:]
        pr = jnp.concatenate([pr_ref[l] for l in range(LB)], axis=-1)
        pooled = (pr + ls_ref[...] * (0.5 * br)) * (1.0 / 64)
        c = pooled - jnp.mean(pooled, axis=-1, keepdims=True)
        v = jnp.mean(c * c, axis=-1, keepdims=True)
        out_ref[...] = (c * lax.rsqrt(v + NORM_EPS)).astype(jnp.bfloat16)

def encode_tiles(x, down, taps, w1, w2, ls):
    nt = x.shape[0]
    one = pl.Buffered(1)
    full = lambda s: pl.BlockSpec(s, lambda g: (0,) * len(s), pipeline_mode=one)
    return pl.pallas_call(
        encode_kernel,
        out_shape=jax.ShapeDtypeStruct((nt, D), jnp.bfloat16),
        grid=(nt // GROUP,),
        in_specs=[
            pl.BlockSpec((GROUP, 16, 16, C_IN), lambda g: (g, 0, 0, 0)),
            full((4 * C_IN, D)), full((KS * KS, D)), full((D, MLP)), full((MLP, D)), full((1, D)),
        ],
        out_specs=pl.BlockSpec((nt, D), lambda g: (0, 0)),
        scratch_shapes=[
            pltpu.VMEM((3, GROUP * PITCH, 128), jnp.float32),
            pltpu.VMEM((64 * GROUP, 4 * C_IN), jnp.bfloat16),
            pltpu.VMEM((LB, 64, GROUP, 128), jnp.float32),
            pltpu.VMEM((LB, 64, GROUP, 128), jnp.float32),
            pltpu.VMEM((64 * GROUP, D), jnp.bfloat16),
            pltpu.VMEM((LB, KS * KS, 8, 128), jnp.float32),
            pltpu.VMEM((nt, MLP), jnp.float32),
            pltpu.VMEM((LB, nt, 128), jnp.float32),
        ],
        compiler_params=pltpu.CompilerParams(vmem_limit_bytes=56 << 20),
        name="encode",
    )(x, down, taps, w1, w2, ls.reshape(1, D))


from jax.sharding import PartitionSpec as P

HEADS = 12
HEAD_DIM = 64
SEQ_DEV = 192
HALF_SEQ = 96
CAP = 2
CODED = D + 128
FAR_NEGATIVE = -1e30
MESH = pl.DeviceIdType.MESH


def row_norm(values):
    center = values - jnp.sum(values, axis=-1, keepdims=True) * (1.0 / D)
    spread = jnp.sum(center * center, axis=-1, keepdims=True) * (1.0 / D)
    return center * lax.rsqrt(spread + NORM_EPS)


def route_kernel(slides, ctxs, out_ref, rows_ref, recv_ref, a2a_send, a2a_recv, own_sem, ring_send, ring_recv):
    count = slides * ctxs
    slide = lax.axis_index("slide")
    ctx = lax.axis_index("ctx")
    me = slide * ctxs + ctx
    barrier = pltpu.get_barrier_semaphore()

    def greet(k, _):
        peer = lax.rem(me + k, count)
        pl.semaphore_signal(barrier, inc=1, device_id=(peer // ctxs, lax.rem(peer, ctxs)), device_id_type=MESH)
        return 0
    lax.fori_loop(1, count, greet, 0)
    pl.semaphore_wait(barrier, count - 1)

    own = pltpu.make_async_copy(out_ref.at[me], recv_ref.at[me], own_sem)
    own.start()

    def send(k, _):
        peer = lax.rem(me + k, count)
        pltpu.make_async_remote_copy(
            src_ref=out_ref.at[peer], dst_ref=recv_ref.at[me], send_sem=a2a_send, recv_sem=a2a_recv,
            device_id=(peer // ctxs, lax.rem(peer, ctxs)), device_id_type=MESH).start()
        return 0
    lax.fori_loop(1, count, send, 0)
    own.wait()
    rest = pl.ds(0, count - 1)
    whole = pltpu.make_async_remote_copy(
        src_ref=out_ref.at[rest], dst_ref=recv_ref.at[rest], send_sem=a2a_send, recv_sem=a2a_recv,
        device_id=(slide, ctx), device_id_type=MESH)
    whole.wait_recv()

    arrived = recv_ref[...].reshape(count * CAP, CODED)
    code = arrived[:, D:].astype(jnp.float32)
    lane = lax.broadcasted_iota(jnp.int32, (count * CAP, 128), 1).astype(jnp.float32) + 1.0
    pick = jnp.concatenate([jnp.where(code == lane, 1.0, 0.0), jnp.where(code == lane + 128.0, 1.0, 0.0)], axis=1)
    mine = lax.dot_general(pick.astype(jnp.bfloat16), arrived[:, :D], (((0,), (0,)), ((), ())),
                           preferred_element_type=jnp.float32)
    rows_ref[ctx] = mine[:SEQ_DEV].astype(jnp.bfloat16)

    right = lax.rem(ctx + 1, ctxs)
    left = lax.rem(ctx + ctxs - 1, ctxs)
    first, second = pl.ds(0, HALF_SEQ), pl.ds(HALF_SEQ, HALF_SEQ)

    def hop(n, block, half, to):
        return pltpu.make_async_remote_copy(
            src_ref=rows_ref.at[block, half], dst_ref=rows_ref.at[block, half],
            send_sem=ring_send.at[n], recv_sem=ring_recv.at[n], device_id=(slide, to), device_id_type=MESH)
    own_hops = [hop(0, ctx, first, right), hop(1, ctx, second, left), hop(2, ctx, second, right), hop(3, ctx, first, left)]
    for h in own_hops:
        h.start()
    own_hops[0].wait_recv()
    onward = hop(4, left, first, right)
    onward.start()
    own_hops[1].wait_recv()
    back = hop(5, right, second, left)
    back.start()
    own_hops[2].wait_recv()
    own_hops[3].wait_recv()
    onward.wait_recv()
    back.wait_recv()
    for h in own_hops + [onward, back]:
        h.wait_send()
    whole.wait_send()


def route(outgoing, slides, ctxs):
    import functools
    count = slides * ctxs
    return pl.pallas_call(
        functools.partial(route_kernel, slides, ctxs),
        out_shape=jax.ShapeDtypeStruct((ctxs, SEQ_DEV, D), jnp.bfloat16),
        in_specs=[pl.BlockSpec(memory_space=pltpu.VMEM)],
        out_specs=pl.BlockSpec(memory_space=pltpu.VMEM),
        scratch_shapes=[
            pltpu.VMEM((count, CAP, CODED), jnp.bfloat16),
            pltpu.SemaphoreType.DMA, pltpu.SemaphoreType.DMA, pltpu.SemaphoreType.DMA,
            pltpu.SemaphoreType.DMA((6,)), pltpu.SemaphoreType.DMA((6,)),
        ],
        compiler_params=pltpu.CompilerParams(collective_id=0, has_side_effects=True),
        name="route",
    )(outgoing)


def attend_kernel(where_ref, rows_ref, wqkv_ref, wout_ref, out_ref, ln_ref, k_ref, v_ref, q_ref, att_ref):
    length = where_ref[0]
    ctx = where_ref[1]
    total = k_ref.shape[0]

    def norm(n, _):
        base = pl.multiple_of(n * 64, 64)
        ln_ref[pl.ds(base, 64), :] = row_norm(rows_ref[pl.ds(base, 64), :].astype(jnp.float32)).astype(jnp.bfloat16)
        return 0
    lax.fori_loop(0, total // 64, norm, 0, unroll=3)
    start = pl.multiple_of(ctx * SEQ_DEV, 64)
    q = jnp.dot(ln_ref[pl.ds(start, SEQ_DEV), :], wqkv_ref[:, :D], preferred_element_type=jnp.float32)
    q_ref[...] = (q.astype(jnp.bfloat16).astype(jnp.float32) * HEAD_DIM ** (-0.5)).astype(jnp.bfloat16)
    k_ref[...] = jnp.dot(ln_ref[...], wqkv_ref[:, D:2 * D], preferred_element_type=jnp.float32).astype(jnp.bfloat16)
    v_ref[...] = jnp.dot(ln_ref[...], wqkv_ref[:, 2 * D:], preferred_element_type=jnp.float32).astype(jnp.bfloat16)
    key = lax.broadcasted_iota(jnp.int32, (1, total), 1)
    bias = jnp.where(key < length, 0.0, FAR_NEGATIVE)
    low = lax.broadcasted_iota(jnp.int32, (SEQ_DEV, 128), 1) < HEAD_DIM
    for pair in range(HEADS // 2):
        cols = slice(pair * 128, pair * 128 + 128)
        q2 = q_ref[:, cols]
        zero = jnp.zeros_like(q2)
        both = jnp.concatenate([jnp.where(low, q2, zero), jnp.where(low, zero, q2)], axis=0)
        s = lax.dot_general(both, k_ref[:, cols], (((1,), (1,)), ((), ())), preferred_element_type=jnp.float32) + bias
        w = jnp.exp(s - jnp.max(s, axis=-1, keepdims=True))
        denom = jnp.sum(w, axis=-1, keepdims=True)
        o = jnp.dot(w.astype(jnp.bfloat16), v_ref[:, cols], preferred_element_type=jnp.float32) / denom
        att_ref[:, cols] = jnp.where(low, o[:SEQ_DEV], o[SEQ_DEV:]).astype(jnp.bfloat16)
    out = jnp.dot(att_ref[...], wout_ref[...], preferred_element_type=jnp.float32)
    out = out + rows_ref[pl.ds(start, SEQ_DEV), :].astype(jnp.float32)
    row = lax.broadcasted_iota(jnp.int32, (SEQ_DEV, 1), 0) + start
    out_ref[...] = jnp.where(row < length, out, 0.0).astype(jnp.bfloat16)


def attend(where, rows, wqkv, wout):
    total = rows.shape[0]
    vmem = pl.BlockSpec(memory_space=pltpu.VMEM)
    return pl.pallas_call(
        attend_kernel,
        out_shape=jax.ShapeDtypeStruct((SEQ_DEV, D), jnp.bfloat16),
        in_specs=[pl.BlockSpec(memory_space=pltpu.SMEM), vmem, vmem, vmem],
        out_specs=vmem,
        scratch_shapes=[
            pltpu.VMEM((total, D), jnp.bfloat16), pltpu.VMEM((total, D), jnp.bfloat16),
            pltpu.VMEM((total, D), jnp.bfloat16), pltpu.VMEM((SEQ_DEV, D), jnp.bfloat16),
            pltpu.VMEM((SEQ_DEV, D), jnp.bfloat16),
        ],
        compiler_params=pltpu.CompilerParams(vmem_limit_bytes=40 << 20),
        name="attend",
    )(where, rows, wqkv, wout)


def shards(feature_maps, down_weight, conv_taps, mlp_in, mlp_out, layer_scale, qkv_weight, out_weight,
           tile_slide, tile_pos, slide_len):
    ctxs = lax.axis_size("ctx")
    slides = lax.axis_size("slide")
    tiles_here = feature_maps.shape[0]
    embeds = encode_tiles(feature_maps, down_weight, conv_taps, mlp_in, mlp_out, layer_scale)
    owner_index = tile_slide * ctxs + tile_pos // SEQ_DEV
    tile_order = jnp.arange(tiles_here, dtype=jnp.int32)
    earlier = (owner_index[None, :] == owner_index[:, None]) & (tile_order[None, :] < tile_order[:, None])
    tile_rank = jnp.sum(earlier.astype(jnp.int32), axis=1)
    target_row = owner_index * CAP + tile_rank
    placing = jnp.arange(slides * ctxs * CAP, dtype=jnp.int32)[:, None] == target_row[None, :]
    slot_code = (tile_pos % SEQ_DEV + 1).astype(jnp.bfloat16)
    coded = jnp.concatenate([embeds, jnp.broadcast_to(slot_code[:, None], (tiles_here, 128))], axis=1)
    outgoing = jnp.dot(placing.astype(jnp.bfloat16), coded, preferred_element_type=jnp.float32).astype(jnp.bfloat16)
    rows = route(outgoing.reshape(slides * ctxs, CAP, CODED), slides, ctxs).reshape(ctxs * SEQ_DEV, D)
    where = jnp.stack([slide_len[lax.axis_index("slide")], lax.axis_index("ctx")])
    return attend(where, rows, qkv_weight[0], out_weight[0])


def solution(mesh):
    whole = P(("slide", "ctx"))
    return jax.shard_map(
        shards,
        mesh=mesh,
        in_specs=(whole, P(), P(), P(), P(), P(), P(), P(), whole, whole, P()),
        out_specs=whole,
        check_vma=False,
    )
```

```python
import functools

import jax
import jax.numpy as jnp
from jax import lax
from jax.experimental import pallas as pl
from jax.experimental.pallas import tpu as pltpu

NORM_EPS = 1e-06
GROUP = 8
HALF = 8
KS = 7
C_IN = 384
D = 768
LB = D // 128
MLP = 3072
HC = 512
PITCH = 257
INV_SQRT2 = 0.7071067811865476


def split_bf16(values):
    high = values.astype(jnp.bfloat16)
    return high, (values - high.astype(jnp.float32)).astype(jnp.bfloat16)


def lane_total(values, ones):
    return jnp.dot(jnp.concatenate(split_bf16(values), axis=-1), ones, preferred_element_type=jnp.float32)


def norm_maps(x_ref, s_ref, g):
    ones = jnp.full((256, 128), 1.0, jnp.bfloat16)
    inv_n = 1.0 / C_IN

    def one_tile(t, _):
        def parts():
            x = x_ref[g * GROUP + t].reshape(256, C_IN)
            return [x[:, l * 128:(l + 1) * 128].astype(jnp.float32) for l in range(3)]
        xs = parts()
        mean = lane_total(xs[0] + xs[1] + xs[2], ones) * inv_n
        cs = [x - mean for x in xs]
        var = lane_total(cs[0] * cs[0] + cs[1] * cs[1] + cs[2] * cs[2], ones) * inv_n
        inv = lax.rsqrt(var + NORM_EPS)
        for l in range(3):
            s_ref[l, pl.ds(t * PITCH, 256), :] = cs[l] * inv
        return 0

    lax.fori_loop(0, GROUP, one_tile, 0, unroll=2)


def make_patches(s_ref, l_ref):
    def patch_rows(n, _):
        i = n // 4
        jp = (n % 4) * 2
        row = pl.multiple_of((i * HALF + jp) * GROUP, 16)
        for dy in range(2):
            for dx in range(2):
                for l in range(3):
                    pos = (2 * i + dy) * 16 + 2 * jp + dx
                    a = s_ref[l, pl.ds(pos, GROUP, stride=PITCH), :]
                    b = s_ref[l, pl.ds(pos + 2, GROUP, stride=PITCH), :]
                    col = (dy * 2 + dx) * C_IN + l * 128
                    l_ref[pl.ds(row, 16), col:col + 128] = jnp.concatenate([a, b], axis=0).astype(jnp.bfloat16)
        return 0
    lax.fori_loop(0, HALF * HALF // 2, patch_rows, 0, unroll=2)


def reduce_chunk(n, l_ref, down_ref, r_ref):
    cols = pl.ds(pl.multiple_of(n * 256, 256), 256)
    red = jnp.dot(l_ref[...], down_ref[:, cols], preferred_element_type=jnp.float32)
    red = red.astype(jnp.bfloat16).astype(jnp.float32)
    for h in range(2):
        r_ref[n * 2 + h] = red[:, h * 128:(h + 1) * 128].reshape(64, GROUP, 128)


def conv_lane(l, r_ref, tap_ref, sp_ref, pr_ref, g):
    psum = None
    for i in range(HALF):
        acc = [None] * HALF
        for a in range(KS):
            ii = i + a - 3
            if not 0 <= ii < HALF:
                continue
            xs = [r_ref[l, ii * HALF + j] for j in range(HALF)]
            for b in range(KS):
                w = tap_ref[l, a * KS + b]
                for j in range(HALF):
                    jj = j + b - 3
                    if 0 <= jj < HALF:
                        term = xs[jj] * w
                        acc[j] = term if acc[j] is None else acc[j] + term
            if ii == i:
                row = ((xs[0] + xs[1]) + (xs[2] + xs[3])) + ((xs[4] + xs[5]) + (xs[6] + xs[7]))
                psum = row if psum is None else psum + row
        for j in range(HALF):
            sp_ref[l, i * HALF + j] = acc[j]
    pr_ref[l, g * GROUP:(g + 1) * GROUP, :] = psum


def norm_spatial(sp_ref, sn_ref):
    def some_rows(n, _):
        rows = [sp_ref[l, pl.ds(n * 8, 8)].reshape(64, 128) for l in range(LB)]
        tot = ((rows[0] + rows[1]) + (rows[2] + rows[3])) + (rows[4] + rows[5])
        mean = jnp.sum(tot, axis=-1, keepdims=True) * (1.0 / D)
        cs = [r - mean for r in rows]
        sq = [c * c for c in cs]
        sq = ((sq[0] + sq[1]) + (sq[2] + sq[3])) + (sq[4] + sq[5])
        inv = lax.rsqrt(jnp.sum(sq, axis=-1, keepdims=True) * (1.0 / D) + NORM_EPS)
        for l in range(LB):
            sn_ref[pl.ds(pl.multiple_of(n * 64, 64), 64), l * 128:(l + 1) * 128] = (cs[l] * inv).astype(jnp.bfloat16)
        return 0
    lax.fori_loop(0, 8, some_rows, 0, unroll=4)


def hidden_chunk(c, sn_ref, w1_ref, ph_ref, g):
    cols = pl.ds(pl.multiple_of(c * HC, HC), HC)
    h = jnp.dot(sn_ref[...], w1_ref[:, cols], preferred_element_type=jnp.float32)
    h = h + h * lax.erf(h * INV_SQRT2)
    ph_ref[g * GROUP:(g + 1) * GROUP, cols] = jnp.sum(h.reshape(64, GROUP, HC), axis=0)


def encode_kernel(groups, x_hbm, down_hbm, taps_ref, w1_hbm, w2_hbm, ls_ref, out_ref,
                  x_ref, down_ref, w1_ref, w2_ref, s_ref, l0_ref, l1_ref, r0_ref, r1_ref, sp_ref, sn_ref, tap_ref, ph_ref, pr_ref, sems):
    l_bufs, r_bufs = (l0_ref, l1_ref), (r0_ref, r1_ref)
    x_copy = [pltpu.make_async_copy(x_hbm.at[pl.ds(g * GROUP, GROUP)], x_ref.at[pl.ds(g * GROUP, GROUP)], sems.at[g])
              for g in range(groups)]
    down_copy = pltpu.make_async_copy(down_hbm, down_ref, sems.at[groups])
    w1_copy = pltpu.make_async_copy(w1_hbm, w1_ref, sems.at[groups + 1])
    w2_copy = pltpu.make_async_copy(w2_hbm, w2_ref, sems.at[groups + 2])
    x_copy[0].start()
    down_copy.start()
    t = taps_ref[...].astype(jnp.float32)
    for k in range(KS * KS):
        for l in range(LB):
            tap_ref[l, k] = jnp.broadcast_to(t[k:k + 1, l * 128:(l + 1) * 128], (8, 128))
    x_copy[0].wait()
    x_copy[1].start()
    w1_copy.start()
    norm_maps(x_ref, s_ref, 0)
    make_patches(s_ref, l0_ref)
    for g in range(2, groups):
        x_copy[g].start()
    w2_copy.start()
    down_copy.wait()

    def first(n, _):
        reduce_chunk(n, l0_ref, down_ref, r0_ref)
        return 0
    lax.fori_loop(0, 3, first, 0)
    x_copy[1].wait()
    norm_maps(x_ref, s_ref, 1)
    make_patches(s_ref, l1_ref)

    for g in range(groups + 1):
        if g == 1:
            w1_copy.wait()

        def step(n, _):
            if g >= 1:
                hidden_chunk(2 * n, sn_ref, w1_ref, ph_ref, g - 1)
            if g < groups:
                conv_lane(2 * n, r_bufs[g % 2], tap_ref, sp_ref, pr_ref, g)
            if g >= 1:
                hidden_chunk(2 * n + 1, sn_ref, w1_ref, ph_ref, g - 1)
            if g < groups:
                conv_lane(2 * n + 1, r_bufs[g % 2], tap_ref, sp_ref, pr_ref, g)
            if g + 1 < groups:
                reduce_chunk(n, l_bufs[(g + 1) % 2], down_ref, r_bufs[(g + 1) % 2])
            return 0
        lax.fori_loop(0, 3, step, 0)
        if g < groups:
            norm_spatial(sp_ref, sn_ref)
        if g + 2 < groups:
            x_copy[g + 2].wait()
            norm_maps(x_ref, s_ref, g + 2)
            make_patches(s_ref, l_bufs[g % 2])

    w2_copy.wait()
    br = jnp.dot(jnp.concatenate(split_bf16(ph_ref[...]), axis=0), w2_ref[...], preferred_element_type=jnp.float32)
    nt = groups * GROUP
    br = br[:nt] + br[nt:]
    pr = jnp.concatenate([pr_ref[l] for l in range(LB)], axis=-1)
    pooled = (pr + ls_ref[...].reshape(1, D) * (0.5 * br)) * (1.0 / (HALF * HALF))
    c = pooled - jnp.mean(pooled, axis=-1, keepdims=True)
    v = jnp.mean(c * c, axis=-1, keepdims=True)
    out_ref[...] = (c * lax.rsqrt(v + NORM_EPS)).astype(jnp.bfloat16)


def encode_tiles(x, down, taps, w1, w2, ls):
    nt = x.shape[0]
    groups = nt // GROUP
    hbm = pl.BlockSpec(memory_space=pl.ANY)
    vmem = pl.BlockSpec(memory_space=pltpu.VMEM)
    return pl.pallas_call(
        functools.partial(encode_kernel, groups),
        out_shape=jax.ShapeDtypeStruct((nt, D), jnp.bfloat16),
        in_specs=[hbm, hbm, vmem, hbm, hbm, vmem],
        out_specs=vmem,
        scratch_shapes=[
            pltpu.VMEM((nt, 16, 16, C_IN), jnp.bfloat16),
            pltpu.VMEM((4 * C_IN, D), jnp.bfloat16),
            pltpu.VMEM((D, MLP), jnp.bfloat16),
            pltpu.VMEM((MLP, D), jnp.bfloat16),
            pltpu.VMEM((3, GROUP * PITCH, 128), jnp.float32),
            pltpu.VMEM((64 * GROUP, 4 * C_IN), jnp.bfloat16),
            pltpu.VMEM((64 * GROUP, 4 * C_IN), jnp.bfloat16),
            pltpu.VMEM((LB, 64, GROUP, 128), jnp.float32),
            pltpu.VMEM((LB, 64, GROUP, 128), jnp.float32),
            pltpu.VMEM((LB, 64, GROUP, 128), jnp.float32),
            pltpu.VMEM((64 * GROUP, D), jnp.bfloat16),
            pltpu.VMEM((LB, KS * KS, 8, 128), jnp.float32),
            pltpu.VMEM((nt, MLP), jnp.float32),
            pltpu.VMEM((LB, nt, 128), jnp.float32),
            pltpu.SemaphoreType.DMA((groups + 3,)),
        ],
        compiler_params=pltpu.CompilerParams(vmem_limit_bytes=56 << 20),
        name="encode",
    )(x, down, taps, w1, w2, ls)


from jax.sharding import PartitionSpec as P

HEADS = 12
HEAD_DIM = 64
SEQ_DEV = 192
HALF_SEQ = 96
CAP = 2
CODED = D + 128
FAR_NEGATIVE = -1e30
MESH = pl.DeviceIdType.MESH


def row_norm(values):
    center = values - jnp.sum(values, axis=-1, keepdims=True) * (1.0 / D)
    spread = jnp.sum(center * center, axis=-1, keepdims=True) * (1.0 / D)
    return center * lax.rsqrt(spread + NORM_EPS)


def tail_kernel(slides, ctxs, emb_ref, slide_ref, pos_ref, len_ref, wqkv_hbm, wout_hbm, out_ref,
                wqkv_ref, wout_ref, send_ref, recv_ref, rows_ref, k_ref, v_ref, q_ref, att_ref,
                load_sem, a2a_send, a2a_recv, own_sem, ring_send, ring_recv):
    count = slides * ctxs
    tiles = emb_ref.shape[0]
    total = ctxs * SEQ_DEV
    slide = lax.axis_index("slide")
    ctx = lax.axis_index("ctx")
    me = slide * ctxs + ctx
    barrier = pltpu.get_barrier_semaphore()

    def greet(k, _):
        peer = lax.rem(me + k, count)
        pl.semaphore_signal(barrier, inc=1, device_id=(peer // ctxs, lax.rem(peer, ctxs)), device_id_type=MESH)
        return 0
    lax.fori_loop(1, count, greet, 0)
    load_qkv = pltpu.make_async_copy(wqkv_hbm, wqkv_ref, load_sem.at[0])
    load_out = pltpu.make_async_copy(wout_hbm, wout_ref, load_sem.at[1])
    load_qkv.start()
    load_out.start()

    pos = pos_ref[...].reshape(1, tiles).astype(jnp.float32)
    block = jnp.floor((pos + 0.5) * (1.0 / SEQ_DEV))
    owner = slide_ref[...].reshape(1, tiles).astype(jnp.float32) * ctxs + block
    code = pos - block * SEQ_DEV + 1.0
    line = lax.broadcasted_iota(jnp.int32, (count * CAP, tiles), 0)
    target = (line // CAP).astype(jnp.float32)
    member = jnp.where(owner == target, 1.0, 0.0)
    before = lax.broadcasted_iota(jnp.int32, (tiles, tiles), 0) < lax.broadcasted_iota(jnp.int32, (tiles, tiles), 1)
    rank = jnp.dot(member.astype(jnp.bfloat16), jnp.where(before, 1.0, 0.0).astype(jnp.bfloat16),
                   preferred_element_type=jnp.float32)
    chosen = jnp.where(rank == (line % CAP).astype(jnp.float32), member, 0.0)
    codes = jnp.broadcast_to(jnp.sum(chosen * code, axis=1, keepdims=True), (count * CAP, 128))
    moved = jnp.dot(chosen.astype(jnp.bfloat16), emb_ref[...], preferred_element_type=jnp.float32)
    send_ref[:, :, :D] = moved.reshape(count, CAP, D).astype(jnp.bfloat16)
    send_ref[:, :, D:] = codes.reshape(count, CAP, 128).astype(jnp.bfloat16)
    pl.semaphore_wait(barrier, count - 1)

    own = pltpu.make_async_copy(send_ref.at[me], recv_ref.at[me], own_sem)
    own.start()

    def send(k, _):
        peer = lax.rem(me + k, count)
        pltpu.make_async_remote_copy(
            src_ref=send_ref.at[peer], dst_ref=recv_ref.at[me], send_sem=a2a_send, recv_sem=a2a_recv,
            device_id=(peer // ctxs, lax.rem(peer, ctxs)), device_id_type=MESH).start()
        return 0
    lax.fori_loop(1, count, send, 0)
    own.wait()
    rest = pl.ds(0, count - 1)
    whole = pltpu.make_async_remote_copy(
        src_ref=send_ref.at[rest], dst_ref=recv_ref.at[rest], send_sem=a2a_send, recv_sem=a2a_recv,
        device_id=(slide, ctx), device_id_type=MESH)
    whole.wait_recv()

    arrived = recv_ref[...].reshape(count * CAP, CODED)
    got = arrived[:, D:].astype(jnp.float32)
    lane = lax.broadcasted_iota(jnp.int32, (count * CAP, 128), 1).astype(jnp.float32) + 1.0
    pick = jnp.concatenate([jnp.where(got == lane, 1.0, 0.0), jnp.where(got == lane + 128.0, 1.0, 0.0)], axis=1)
    mine = lax.dot_general(pick.astype(jnp.bfloat16), arrived[:, :D], (((0,), (0,)), ((), ())),
                           preferred_element_type=jnp.float32)
    rows_ref[ctx] = mine[:SEQ_DEV].astype(jnp.bfloat16)

    right = lax.rem(ctx + 1, ctxs)
    left = lax.rem(ctx + ctxs - 1, ctxs)
    far = lax.rem(ctx + 2, ctxs)
    first, second = pl.ds(0, HALF_SEQ), pl.ds(HALF_SEQ, HALF_SEQ)

    def hop(n, blk, half, to):
        return pltpu.make_async_remote_copy(
            src_ref=rows_ref.at[blk, half], dst_ref=rows_ref.at[blk, half],
            send_sem=ring_send.at[n], recv_sem=ring_recv.at[n], device_id=(slide, to), device_id_type=MESH)

    def keys_values(blk):
        ln = row_norm(rows_ref[blk].astype(jnp.float32)).astype(jnp.bfloat16)
        at = pl.ds(pl.multiple_of(blk * SEQ_DEV, 64), SEQ_DEV)
        k_ref[at, :] = jnp.dot(ln, wqkv_ref[:, D:2 * D], preferred_element_type=jnp.float32).astype(jnp.bfloat16)
        v_ref[at, :] = jnp.dot(ln, wqkv_ref[:, 2 * D:], preferred_element_type=jnp.float32).astype(jnp.bfloat16)
        return ln
    own_hops = [hop(0, ctx, first, right), hop(1, ctx, second, left), hop(2, ctx, second, right), hop(3, ctx, first, left)]
    for h in own_hops:
        h.start()
    load_qkv.wait()
    ln = keys_values(ctx)
    q = jnp.dot(ln, wqkv_ref[:, :D], preferred_element_type=jnp.float32)
    q_ref[...] = (q.astype(jnp.bfloat16).astype(jnp.float32) * HEAD_DIM ** (-0.5)).astype(jnp.bfloat16)
    own_hops[0].wait_recv()
    onward = hop(4, left, first, right)
    onward.start()
    own_hops[1].wait_recv()
    back = hop(5, right, second, left)
    back.start()
    own_hops[2].wait_recv()
    own_hops[3].wait_recv()

    def near(n, _):
        keys_values(lax.rem(ctx + 1 + 2 * n, ctxs))
        return 0
    lax.fori_loop(0, 2, near, 0)
    onward.wait_recv()
    back.wait_recv()
    keys_values(far)
    for h in own_hops + [onward, back]:
        h.wait_send()
    whole.wait_send()
    load_out.wait()

    length = len_ref[slide]
    key = lax.broadcasted_iota(jnp.int32, (1, total), 1)
    bias = jnp.where(key < length, 0.0, FAR_NEGATIVE)
    low = lax.broadcasted_iota(jnp.int32, (SEQ_DEV, 128), 1) < HEAD_DIM
    for pair in range(HEADS // 2):
        cols = slice(pair * 128, pair * 128 + 128)
        q2 = q_ref[:, cols]
        zero = jnp.zeros_like(q2)
        both = jnp.concatenate([jnp.where(low, q2, zero), jnp.where(low, zero, q2)], axis=0)
        s = lax.dot_general(both, k_ref[:, cols], (((1,), (1,)), ((), ())), preferred_element_type=jnp.float32) + bias
        w = jnp.exp(s - jnp.max(s, axis=-1, keepdims=True))
        denom = jnp.sum(w, axis=-1, keepdims=True)
        o = jnp.dot(w.astype(jnp.bfloat16), v_ref[:, cols], preferred_element_type=jnp.float32) / denom
        att_ref[:, cols] = jnp.where(low, o[:SEQ_DEV], o[SEQ_DEV:]).astype(jnp.bfloat16)
    out = jnp.dot(att_ref[...], wout_ref[...], preferred_element_type=jnp.float32)
    out = out + rows_ref[ctx].astype(jnp.float32)
    row = lax.broadcasted_iota(jnp.int32, (SEQ_DEV, 1), 0) + ctx * SEQ_DEV
    out_ref[...] = jnp.where(row < length, out, 0.0).astype(jnp.bfloat16)


def slide_layer(embeds, tile_slide, tile_pos, slide_len, wqkv, wout, slides, ctxs):
    count = slides * ctxs
    total = ctxs * SEQ_DEV
    vmem = pl.BlockSpec(memory_space=pltpu.VMEM)
    hbm = pl.BlockSpec(memory_space=pl.ANY)
    return pl.pallas_call(
        functools.partial(tail_kernel, slides, ctxs),
        out_shape=jax.ShapeDtypeStruct((SEQ_DEV, D), jnp.bfloat16),
        in_specs=[vmem, vmem, vmem, pl.BlockSpec(memory_space=pltpu.SMEM), hbm, hbm],
        out_specs=vmem,
        scratch_shapes=[
            pltpu.VMEM((D, 3 * D), jnp.bfloat16), pltpu.VMEM((D, D), jnp.bfloat16),
            pltpu.VMEM((count, CAP, CODED), jnp.bfloat16), pltpu.VMEM((count, CAP, CODED), jnp.bfloat16),
            pltpu.VMEM((ctxs, SEQ_DEV, D), jnp.bfloat16),
            pltpu.VMEM((total, D), jnp.bfloat16), pltpu.VMEM((total, D), jnp.bfloat16),
            pltpu.VMEM((SEQ_DEV, D), jnp.bfloat16), pltpu.VMEM((SEQ_DEV, D), jnp.bfloat16),
            pltpu.SemaphoreType.DMA((2,)),
            pltpu.SemaphoreType.DMA, pltpu.SemaphoreType.DMA, pltpu.SemaphoreType.DMA,
            pltpu.SemaphoreType.DMA((6,)), pltpu.SemaphoreType.DMA((6,)),
        ],
        compiler_params=pltpu.CompilerParams(collective_id=0, has_side_effects=True, vmem_limit_bytes=48 << 20),
        name="slide_layer",
    )(embeds, tile_slide, tile_pos, slide_len, wqkv, wout)


def shards(feature_maps, down_weight, conv_taps, mlp_in, mlp_out, layer_scale, qkv_weight, out_weight,
           tile_slide, tile_pos, slide_len):
    embeds = encode_tiles(feature_maps, down_weight, conv_taps, mlp_in, mlp_out, layer_scale)
    return slide_layer(embeds, tile_slide, tile_pos, slide_len, qkv_weight[0], out_weight[0],
                       lax.axis_size("slide"), lax.axis_size("ctx"))


def solution(mesh):
    whole = P(("slide", "ctx"))
    return jax.shard_map(
        shards,
        mesh=mesh,
        in_specs=(whole, P(), P(), P(), P(), P(), P(), P(), whole, whole, P()),
        out_specs=whole,
        check_vma=False,
    )
```

```python
import functools

import jax
import jax.numpy as jnp
from jax import lax
from jax.experimental import pallas as pl
from jax.experimental.pallas import tpu as pltpu
from jax.sharding import PartitionSpec as P

NORM_EPS = 1e-06
GROUP = 8
HALF = 8
KS = 7
C_IN = 384
D = 768
LB = D // 128
MLP = 3072
HC = 512
PITCH = 257
INV_SQRT2 = 0.7071067811865476
BSPLIT = 2


def split_bf16(values):
    high = values.astype(jnp.bfloat16)
    return high, (values - high.astype(jnp.float32)).astype(jnp.bfloat16)


def norm_rows(n, x_ref, s_ref, g):
    t = n // 4
    y = (n % 4) * 4
    x = x_ref[g * GROUP + t, pl.ds(y, 4)].reshape(64, C_IN).astype(jnp.float32)
    c = x - jnp.sum(x, axis=-1, keepdims=True) * (1.0 / C_IN)
    v = jnp.sum(c * c, axis=-1, keepdims=True) * (1.0 / C_IN)
    o = c * lax.rsqrt(v + NORM_EPS)
    for l in range(3):
        s_ref[l, pl.ds(t * PITCH + y * 16, 64), :] = o[:, l * 128:(l + 1) * 128]


def make_patches(s_ref, l_ref):
    def patch_rows(n, _):
        i = n // 4
        jp = (n % 4) * 2
        row = pl.multiple_of((i * HALF + jp) * GROUP, 16)
        for dy in range(2):
            for dx in range(2):
                for l in range(3):
                    pos = (2 * i + dy) * 16 + 2 * jp + dx
                    a = s_ref[l, pl.ds(pos, GROUP, stride=PITCH), :]
                    b = s_ref[l, pl.ds(pos + 2, GROUP, stride=PITCH), :]
                    col = (dy * 2 + dx) * C_IN + l * 128
                    l_ref[pl.ds(row, 16), col:col + 128] = jnp.concatenate([a, b], axis=0).astype(jnp.bfloat16)
        return 0
    lax.fori_loop(0, HALF * HALF // 2, patch_rows, 0, unroll=2)


def reduce_rows(m, l_ref, down_ref, r_ref):
    rows = 64 * GROUP // BSPLIT
    lhs = l_ref[pl.ds(pl.multiple_of(m * rows, rows), rows), :]
    red = jnp.dot(lhs, down_ref[...], preferred_element_type=jnp.float32)
    red = red.astype(jnp.bfloat16).astype(jnp.float32)
    for h in range(LB):
        r_ref[h, pl.ds(m * (rows // GROUP), rows // GROUP)] = red[:, h * 128:(h + 1) * 128].reshape(rows // GROUP, GROUP, 128)


def conv_lane(l, r_ref, tap_ref, sp_ref, pr_ref, g):
    psum = None
    for i in range(HALF):
        acc = [None] * HALF
        for a in range(KS):
            ii = i + a - 3
            if not 0 <= ii < HALF:
                continue
            xs = [r_ref[l, ii * HALF + j] for j in range(HALF)]
            for b in range(KS):
                w = tap_ref[l, a * KS + b]
                for j in range(HALF):
                    jj = j + b - 3
                    if 0 <= jj < HALF:
                        term = xs[jj] * w
                        acc[j] = term if acc[j] is None else acc[j] + term
            if ii == i:
                row = ((xs[0] + xs[1]) + (xs[2] + xs[3])) + ((xs[4] + xs[5]) + (xs[6] + xs[7]))
                psum = row if psum is None else psum + row
        for j in range(HALF):
            sp_ref[l, i * HALF + j] = acc[j]
    pr_ref[l, g * GROUP:(g + 1) * GROUP, :] = psum


def norm_spatial(sp_ref, sn_ref):
    def some_rows(n, _):
        rows = [sp_ref[l, pl.ds(n * 8, 8)].reshape(64, 128) for l in range(LB)]
        tot = ((rows[0] + rows[1]) + (rows[2] + rows[3])) + (rows[4] + rows[5])
        mean = jnp.sum(tot, axis=-1, keepdims=True) * (1.0 / D)
        cs = [r - mean for r in rows]
        sq = [c * c for c in cs]
        sq = ((sq[0] + sq[1]) + (sq[2] + sq[3])) + (sq[4] + sq[5])
        inv = lax.rsqrt(jnp.sum(sq, axis=-1, keepdims=True) * (1.0 / D) + NORM_EPS) * INV_SQRT2
        for l in range(LB):
            sn_ref[pl.ds(pl.multiple_of(n * 64, 64), 64), l * 128:(l + 1) * 128] = (cs[l] * inv).astype(jnp.bfloat16)
        return 0
    lax.fori_loop(0, 8, some_rows, 0, unroll=8)


def hidden_chunk(c, sn_ref, w1_ref, ph_ref, g):
    h = jnp.dot(sn_ref[...], w1_ref[c], preferred_element_type=jnp.float32)
    h = h + h * lax.erf(h)
    ph_ref[c, g * GROUP:(g + 1) * GROUP, :] = jnp.sum(h.reshape(64, GROUP, HC), axis=0)


def encode(groups, more_loads, x_hbm, down_hbm, taps_ref, w1_hbm, w2_hbm, ls_ref, emb_ref,
                  x_ref, down_ref, w1_ref, w2_ref, s_ref, l0_ref, l1_ref, r0_ref, r1_ref, sp_ref, sn_ref, tap_ref, ph_ref, pr_ref, sems):
    l_bufs, r_bufs = (l0_ref, l1_ref), (r0_ref, r1_ref)
    x_copy = [pltpu.make_async_copy(x_hbm.at[pl.ds(g * GROUP, GROUP)], x_ref.at[pl.ds(g * GROUP, GROUP)], sems.at[g])
              for g in range(groups)]
    down_copy = pltpu.make_async_copy(down_hbm, down_ref, sems.at[groups])
    w1_copy = [pltpu.make_async_copy(w1_hbm.at[:, pl.ds(c * HC, HC)], w1_ref.at[c], sems.at[groups + 2 + c]) for c in range(LB)]
    w2_copy = pltpu.make_async_copy(w2_hbm, w2_ref, sems.at[groups + 1])
    x_copy[0].start()
    down_copy.start()
    t = taps_ref[...].astype(jnp.float32)
    for k in range(KS * KS):
        for l in range(LB):
            tap_ref[l, k] = jnp.broadcast_to(t[k:k + 1, l * 128:(l + 1) * 128], (8, 128))
    x_copy[0].wait()
    x_copy[1].start()
    for copy in w1_copy:
        copy.start()
    def only_norm(n, _):
        norm_rows(n, x_ref, s_ref, 0)
        return 0
    lax.fori_loop(0, GROUP * 4, only_norm, 0, unroll=8)
    make_patches(s_ref, l0_ref)
    for g in range(2, groups):
        x_copy[g].start()
    w2_copy.start()
    for copy in more_loads:
        copy.start()
    down_copy.wait()

    def norm_and_reduce(g_norm, g_red):
        per = GROUP * 4 // BSPLIT

        def step(n, _):
            if g_norm < groups:
                for k in range(per):
                    norm_rows(n * per + k, x_ref, s_ref, g_norm)
            if g_red < groups:
                reduce_rows(n, l_bufs[g_red % 2], down_ref, r_bufs[g_red % 2])
            return 0
        if g_norm < groups:
            x_copy[g_norm].wait()
        lax.fori_loop(0, BSPLIT, step, 0)
        if g_norm < groups:
            make_patches(s_ref, l_bufs[g_norm % 2])
    norm_and_reduce(1, 0)

    for g in range(groups + 1):
        if g == 1:
            for copy in w1_copy:
                copy.wait()

        def step(n, _):
            if g < groups:
                conv_lane(n, r_bufs[g % 2], tap_ref, sp_ref, pr_ref, g)
            if g >= 1:
                hidden_chunk(n, sn_ref, w1_ref, ph_ref, g - 1)
            return 0
        lax.fori_loop(0, LB, step, 0, unroll=3 if g == groups else 1)
        if g < groups:
            norm_spatial(sp_ref, sn_ref)
        if g + 1 < groups:
            norm_and_reduce(g + 2, g + 1)

    w2_copy.wait()
    br = jnp.dot(jnp.concatenate(split_bf16(jnp.concatenate([ph_ref[c] for c in range(LB)], axis=-1)), axis=0), w2_ref[...], preferred_element_type=jnp.float32)
    nt = groups * GROUP
    br = br[:nt] + br[nt:]
    pr = jnp.concatenate([pr_ref[l] for l in range(LB)], axis=-1)
    pooled = (pr + ls_ref[...].reshape(1, D) * (INV_SQRT2 * br)) * (1.0 / (HALF * HALF))
    c = pooled - jnp.mean(pooled, axis=-1, keepdims=True)
    v = jnp.mean(c * c, axis=-1, keepdims=True)
    emb_ref[...] = (c * lax.rsqrt(v + NORM_EPS)).astype(jnp.bfloat16)


HEADS = 12
HEAD_DIM = 64
SEQ_DEV = 192
HALF_SEQ = 96
CAP = 2
CODED = D + 128
FAR_NEGATIVE = -1e30
MESH = pl.DeviceIdType.MESH


def row_norm(values):
    center = values - jnp.sum(values, axis=-1, keepdims=True) * (1.0 / D)
    spread = jnp.sum(center * center, axis=-1, keepdims=True) * (1.0 / D)
    return center * lax.rsqrt(spread + NORM_EPS)


def greet(slides, ctxs):
    count = slides * ctxs
    me = lax.axis_index("slide") * ctxs + lax.axis_index("ctx")
    barrier = pltpu.get_barrier_semaphore()

    def one(k, _):
        peer = lax.rem(me + k, count)
        pl.semaphore_signal(barrier, inc=1, device_id=(peer // ctxs, lax.rem(peer, ctxs)), device_id_type=MESH)
        return 0
    lax.fori_loop(1, count, one, 0)


def slide_layer(slides, ctxs, loads, emb_ref, slide_ref, pos_ref, len_ref, out_ref,
                wqkv_ref, wout_ref, send_ref, recv_ref, rows_ref, k_ref, v_ref, q_ref, att_ref,
                a2a_send, a2a_recv, own_sem, ring_send, ring_recv):
    load_qkv, load_out = loads
    count = slides * ctxs
    tiles = emb_ref.shape[0]
    total = ctxs * SEQ_DEV
    slide = lax.axis_index("slide")
    ctx = lax.axis_index("ctx")
    me = slide * ctxs + ctx
    pos = pos_ref[...].reshape(1, tiles).astype(jnp.float32)
    block = jnp.floor((pos + 0.5) * (1.0 / SEQ_DEV))
    owner = slide_ref[...].reshape(1, tiles).astype(jnp.float32) * ctxs + block
    code = pos - block * SEQ_DEV + 1.0
    line = lax.broadcasted_iota(jnp.int32, (count * CAP, tiles), 0)
    target = (line // CAP).astype(jnp.float32)
    member = jnp.where(owner == target, 1.0, 0.0)
    before = lax.broadcasted_iota(jnp.int32, (tiles, tiles), 0) < lax.broadcasted_iota(jnp.int32, (tiles, tiles), 1)
    rank = jnp.dot(member.astype(jnp.bfloat16), jnp.where(before, 1.0, 0.0).astype(jnp.bfloat16),
                   preferred_element_type=jnp.float32)
    chosen = jnp.where(rank == (line % CAP).astype(jnp.float32), member, 0.0)
    codes = jnp.broadcast_to(jnp.sum(chosen * code, axis=1, keepdims=True), (count * CAP, 128))
    moved = jnp.dot(chosen.astype(jnp.bfloat16), emb_ref[...], preferred_element_type=jnp.float32)
    send_ref[:, :, :D] = moved.reshape(count, CAP, D).astype(jnp.bfloat16)
    send_ref[:, :, D:] = codes.reshape(count, CAP, 128).astype(jnp.bfloat16)
    pl.semaphore_wait(pltpu.get_barrier_semaphore(), count - 1)

    own = pltpu.make_async_copy(send_ref.at[me], recv_ref.at[me], own_sem)
    own.start()

    def send(k, _):
        peer = lax.rem(me + k, count)
        pltpu.make_async_remote_copy(
            src_ref=send_ref.at[peer], dst_ref=recv_ref.at[me], send_sem=a2a_send, recv_sem=a2a_recv,
            device_id=(peer // ctxs, lax.rem(peer, ctxs)), device_id_type=MESH).start()
        return 0
    lax.fori_loop(1, count, send, 0)
    own.wait()
    rest = pl.ds(0, count - 1)
    whole = pltpu.make_async_remote_copy(
        src_ref=send_ref.at[rest], dst_ref=recv_ref.at[rest], send_sem=a2a_send, recv_sem=a2a_recv,
        device_id=(slide, ctx), device_id_type=MESH)
    whole.wait_recv()

    arrived = recv_ref[...].reshape(count * CAP, CODED)
    got = arrived[:, D:].astype(jnp.float32)
    lane = lax.broadcasted_iota(jnp.int32, (count * CAP, 128), 1).astype(jnp.float32) + 1.0
    pick = jnp.concatenate([jnp.where(got == lane, 1.0, 0.0), jnp.where(got == lane + 128.0, 1.0, 0.0)], axis=1)
    mine = lax.dot_general(pick.astype(jnp.bfloat16), arrived[:, :D], (((0,), (0,)), ((), ())),
                           preferred_element_type=jnp.float32)
    rows_ref[ctx] = mine[:SEQ_DEV].astype(jnp.bfloat16)

    right = lax.rem(ctx + 1, ctxs)
    left = lax.rem(ctx + ctxs - 1, ctxs)
    far = lax.rem(ctx + 2, ctxs)
    first, second = pl.ds(0, HALF_SEQ), pl.ds(HALF_SEQ, HALF_SEQ)

    def hop(n, blk, half, to):
        return pltpu.make_async_remote_copy(
            src_ref=rows_ref.at[blk, half], dst_ref=rows_ref.at[blk, half],
            send_sem=ring_send.at[n], recv_sem=ring_recv.at[n], device_id=(slide, to), device_id_type=MESH)

    def keys_values(blk):
        ln = row_norm(rows_ref[blk].astype(jnp.float32)).astype(jnp.bfloat16)
        at = pl.ds(pl.multiple_of(blk * SEQ_DEV, 64), SEQ_DEV)
        k_ref[at, :] = jnp.dot(ln, wqkv_ref[:, D:2 * D], preferred_element_type=jnp.float32).astype(jnp.bfloat16)
        v_ref[at, :] = jnp.dot(ln, wqkv_ref[:, 2 * D:], preferred_element_type=jnp.float32).astype(jnp.bfloat16)
        return ln
    own_hops = [hop(0, ctx, first, right), hop(1, ctx, second, left), hop(2, ctx, second, right), hop(3, ctx, first, left)]
    for h in own_hops:
        h.start()
    load_qkv.wait()
    ln = keys_values(ctx)
    q = jnp.dot(ln, wqkv_ref[:, :D], preferred_element_type=jnp.float32)
    q_ref[...] = (q.astype(jnp.bfloat16).astype(jnp.float32) * HEAD_DIM ** (-0.5)).astype(jnp.bfloat16)
    own_hops[0].wait_recv()
    onward = hop(4, left, first, right)
    onward.start()
    own_hops[1].wait_recv()
    back = hop(5, right, second, left)
    back.start()
    own_hops[2].wait_recv()
    own_hops[3].wait_recv()

    def near(n, _):
        keys_values(lax.rem(ctx + 1 + 2 * n, ctxs))
        return 0
    lax.fori_loop(0, 2, near, 0)
    onward.wait_recv()
    back.wait_recv()
    keys_values(far)
    for h in own_hops + [onward, back]:
        h.wait_send()
    whole.wait_send()
    load_out.wait()

    length = len_ref[slide]
    key = lax.broadcasted_iota(jnp.int32, (1, total), 1)
    bias = jnp.where(key < length, 0.0, FAR_NEGATIVE)
    low = lax.broadcasted_iota(jnp.int32, (SEQ_DEV, 128), 1) < HEAD_DIM
    for pair in range(HEADS // 2):
        cols = slice(pair * 128, pair * 128 + 128)
        q2 = q_ref[:, cols]
        zero = jnp.zeros_like(q2)
        both = jnp.concatenate([jnp.where(low, q2, zero), jnp.where(low, zero, q2)], axis=0)
        s = lax.dot_general(both, k_ref[:, cols], (((1,), (1,)), ((), ())), preferred_element_type=jnp.float32) + bias
        w = jnp.exp(s - jnp.max(s, axis=-1, keepdims=True))
        denom = jnp.sum(w, axis=-1, keepdims=True)
        o = jnp.dot(w.astype(jnp.bfloat16), v_ref[:, cols], preferred_element_type=jnp.float32) / denom
        att_ref[:, cols] = jnp.where(low, o[:SEQ_DEV], o[SEQ_DEV:]).astype(jnp.bfloat16)
    out = jnp.dot(att_ref[...], wout_ref[...], preferred_element_type=jnp.float32)
    out = out + rows_ref[ctx].astype(jnp.float32)
    row = lax.broadcasted_iota(jnp.int32, (SEQ_DEV, 1), 0) + ctx * SEQ_DEV
    out_ref[...] = jnp.where(row < length, out, 0.0).astype(jnp.bfloat16)


def whole_kernel(groups, slides, ctxs, x_hbm, down_hbm, taps_ref, w1_hbm, w2_hbm, ls_ref, wqkv_hbm, wout_hbm,
                 slide_ref, pos_ref, len_ref, out_ref, emb_ref, load_sem, wqkv_ref, wout_ref, send_ref, recv_ref, rows_ref,
                 k_ref, v_ref, q_ref, att_ref, a2a_send, a2a_recv, own_sem, ring_send, ring_recv, *encoder_refs):
    greet(slides, ctxs)
    loads = (pltpu.make_async_copy(wqkv_hbm, wqkv_ref, load_sem.at[0]), pltpu.make_async_copy(wout_hbm, wout_ref, load_sem.at[1]))
    encode(groups, loads, x_hbm, down_hbm, taps_ref, w1_hbm, w2_hbm, ls_ref, emb_ref, *encoder_refs)
    slide_layer(slides, ctxs, loads, emb_ref, slide_ref, pos_ref, len_ref, out_ref,
                wqkv_ref, wout_ref, send_ref, recv_ref, rows_ref, k_ref, v_ref, q_ref, att_ref,
                a2a_send, a2a_recv, own_sem, ring_send, ring_recv)


def shards(x, down, taps, w1, w2, ls, qkv_weight, out_weight, tile_slide, tile_pos, slide_len):
    slides, ctxs = lax.axis_size("slide"), lax.axis_size("ctx")
    nt = x.shape[0]
    groups = nt // GROUP
    count = slides * ctxs
    total = ctxs * SEQ_DEV
    hbm = pl.BlockSpec(memory_space=pl.ANY)
    vmem = pl.BlockSpec(memory_space=pltpu.VMEM)
    return pl.pallas_call(
        functools.partial(whole_kernel, groups, slides, ctxs),
        out_shape=jax.ShapeDtypeStruct((SEQ_DEV, D), jnp.bfloat16),
        in_specs=[hbm, hbm, vmem, hbm, hbm, vmem, hbm, hbm, vmem, vmem, pl.BlockSpec(memory_space=pltpu.SMEM)],
        out_specs=vmem,
        scratch_shapes=[
            pltpu.VMEM((nt, D), jnp.bfloat16), pltpu.SemaphoreType.DMA((2,)),
            pltpu.VMEM((D, 3 * D), jnp.bfloat16), pltpu.VMEM((D, D), jnp.bfloat16),
            pltpu.VMEM((count, CAP, CODED), jnp.bfloat16), pltpu.VMEM((count, CAP, CODED), jnp.bfloat16),
            pltpu.VMEM((ctxs, SEQ_DEV, D), jnp.bfloat16),
            pltpu.VMEM((total, D), jnp.bfloat16), pltpu.VMEM((total, D), jnp.bfloat16),
            pltpu.VMEM((SEQ_DEV, D), jnp.bfloat16), pltpu.VMEM((SEQ_DEV, D), jnp.bfloat16),
            pltpu.SemaphoreType.DMA, pltpu.SemaphoreType.DMA, pltpu.SemaphoreType.DMA,
            pltpu.SemaphoreType.DMA((6,)), pltpu.SemaphoreType.DMA((6,)),
            pltpu.VMEM((nt, 16, 16, C_IN), jnp.bfloat16),
            pltpu.VMEM((4 * C_IN, D), jnp.bfloat16),
            pltpu.VMEM((LB, D, HC), jnp.bfloat16),
            pltpu.VMEM((MLP, D), jnp.bfloat16),
            pltpu.VMEM((3, GROUP * PITCH, 128), jnp.float32),
            pltpu.VMEM((64 * GROUP, 4 * C_IN), jnp.bfloat16),
            pltpu.VMEM((64 * GROUP, 4 * C_IN), jnp.bfloat16),
            pltpu.VMEM((LB, 64, GROUP, 128), jnp.float32),
            pltpu.VMEM((LB, 64, GROUP, 128), jnp.float32),
            pltpu.VMEM((LB, 64, GROUP, 128), jnp.float32),
            pltpu.VMEM((64 * GROUP, D), jnp.bfloat16),
            pltpu.VMEM((LB, KS * KS, 8, 128), jnp.float32),
            pltpu.VMEM((LB, nt, HC), jnp.float32),
            pltpu.VMEM((LB, nt, 128), jnp.float32),
            pltpu.SemaphoreType.DMA((groups + 2 + LB,)),
        ],
        compiler_params=pltpu.CompilerParams(collective_id=0, has_side_effects=True, vmem_limit_bytes=60 << 20),
        name="whole",
    )(x, down, taps, w1, w2, ls, qkv_weight[0], out_weight[0], tile_slide, tile_pos, slide_len)


def solution(mesh):
    whole = P(("slide", "ctx"))
    return jax.shard_map(
        shards,
        mesh=mesh,
        in_specs=(whole, P(), P(), P(), P(), P(), P(), P(), whole, whole, P()),
        out_specs=whole,
        check_vma=False,
    )
```

```python
import functools

import jax
import jax.numpy as jnp
from jax import lax
from jax.experimental import pallas as pl
from jax.experimental.pallas import tpu as pltpu
from jax.sharding import PartitionSpec as P

NORM_EPS = 1e-06
GROUP = 8
HALF = 8
KS = 7
C_IN = 384
D = 768
LB = D // 128
MLP = 3072
HC = 512
PITCH = 257
INV_SQRT2 = 0.7071067811865476
BSPLIT = 2


def split_bf16(values):
    high = values.astype(jnp.bfloat16)
    return high, (values - high.astype(jnp.float32)).astype(jnp.bfloat16)


def norm_rows(n, x_ref, s_ref, g):
    t = n // 4
    y = (n % 4) * 4
    x = x_ref[g * GROUP + t, pl.ds(y, 4)].reshape(64, C_IN).astype(jnp.float32)
    c = x - jnp.sum(x, axis=-1, keepdims=True) * (1.0 / C_IN)
    v = jnp.sum(c * c, axis=-1, keepdims=True) * (1.0 / C_IN)
    o = c * lax.rsqrt(v + NORM_EPS)
    for l in range(3):
        s_ref[l, pl.ds(t * PITCH + y * 16, 64), :] = o[:, l * 128:(l + 1) * 128]


def make_patches(s_ref, l_ref):
    def patch_rows(n, _):
        i = n // 4
        jp = (n % 4) * 2
        row = pl.multiple_of((i * HALF + jp) * GROUP, 16)
        for dy in range(2):
            for dx in range(2):
                for l in range(3):
                    pos = (2 * i + dy) * 16 + 2 * jp + dx
                    a = s_ref[l, pl.ds(pos, GROUP, stride=PITCH), :]
                    b = s_ref[l, pl.ds(pos + 2, GROUP, stride=PITCH), :]
                    col = (dy * 2 + dx) * C_IN + l * 128
                    l_ref[pl.ds(row, 16), col:col + 128] = jnp.concatenate([a, b], axis=0).astype(jnp.bfloat16)
        return 0
    lax.fori_loop(0, HALF * HALF // 2, patch_rows, 0, unroll=2)


def reduce_rows(m, l_ref, down_ref, r_ref):
    rows = 64 * GROUP // BSPLIT
    lhs = l_ref[pl.ds(pl.multiple_of(m * rows, rows), rows), :]
    red = jnp.dot(lhs, down_ref[...], preferred_element_type=jnp.float32)
    red = red.astype(jnp.bfloat16).astype(jnp.float32)
    for h in range(LB):
        r_ref[h, pl.ds(m * (rows // GROUP), rows // GROUP)] = red[:, h * 128:(h + 1) * 128].reshape(rows // GROUP, GROUP, 128)


def tap_axis(part):
    odd = {k: (2 * k + 3,) for k in (-1, 0, 1)}
    even = {k: (2 * k + 2,) for k in (-1, 0, 1, 2)}
    if part == 0:
        return odd
    if part == 1:
        return even
    return {k: even[k] + odd.get(k, ()) for k in even}


TAP_SUMS = []
TAP_AT = {}
for _p in range(3):
    for _q in range(3):
        for _k, _ra in tap_axis(_p).items():
            for _l, _cb in tap_axis(_q).items():
                TAP_AT[(_p, _q, _k, _l)] = len(TAP_SUMS)
                TAP_SUMS.append([a * KS + b for a in _ra for b in _cb])


def fill_taps(taps_ref, tap_ref):
    t = taps_ref[...].astype(jnp.float32)
    for n, sums in enumerate(TAP_SUMS):
        row = t[sums[0]:sums[0] + 1]
        for k in sums[1:]:
            row = row + t[k:k + 1]
        for l in range(LB):
            tap_ref[l, n] = jnp.broadcast_to(row[:, l * 128:(l + 1) * 128], (8, 128))


def conv_lane(l, r_ref, tap_ref, sp_ref, pr_ref, x_tmp, y_tmp, g):
    spots = range(4)
    psum = None
    for i in range(HALF):
        xs = [r_ref[l, i * HALF + j] for j in range(HALF)]
        for j in spots:
            x_tmp[i, 2, j] = xs[2 * j] + xs[2 * j + 1]
    for i in spots:
        row = None
        for q in range(3):
            for j in spots:
                top = r_ref[l, 2 * i * HALF + 2 * j + q] if q < 2 else x_tmp[2 * i, 2, j]
                low = r_ref[l, (2 * i + 1) * HALF + 2 * j + q] if q < 2 else x_tmp[2 * i + 1, 2, j]
                both = top + low
                x_tmp[8 + i, q, j] = both
                if q == 2:
                    row = both if row is None else row + both
        psum = row if psum is None else psum + row
    pr_ref[l, g * GROUP:(g + 1) * GROUP, :] = psum

    def load(p, q, i, j):
        if p == 2:
            return x_tmp[8 + i, q, j]
        if q == 2:
            return x_tmp[2 * i + p, 2, j]
        return r_ref[l, (2 * i + p) * HALF + 2 * j + q]

    outs = [range(4), range(-1, 4), range(4)]
    base = [0, 5, 9]
    for p in range(3):
        for i in outs[p]:
            part = []
            for q in range(3):
                acc = {}
                for k in tap_axis(p):
                    if not 0 <= i + k < 4:
                        continue
                    xs = [load(p, q, i + k, j) for j in spots]
                    for m in tap_axis(q):
                        w = tap_ref[l, TAP_AT[(p, q, k, m)]]
                        for j in outs[q]:
                            if 0 <= j + m < 4:
                                term = xs[j + m] * w
                                acc[j] = acc[j] + term if j in acc else term
                part.append(acc)
            for j in spots:
                y_tmp[base[p] + i, 2 * j] = part[0][j] + part[1][j - 1]
                y_tmp[base[p] + i, 2 * j + 1] = part[2][j] - part[0][j] - part[1][j]
    for i in spots:
        for j in range(HALF):
            a, b, before, c = y_tmp[i, j], y_tmp[5 + i, j], y_tmp[4 + i, j], y_tmp[9 + i, j]
            sp_ref[l, 2 * i * HALF + j] = a + before
            sp_ref[l, (2 * i + 1) * HALF + j] = c - a - b


def norm_spatial(sp_ref, sn_ref):
    def some_rows(n, _):
        rows = [sp_ref[l, pl.ds(n * 8, 8)].reshape(64, 128) for l in range(LB)]
        tot = ((rows[0] + rows[1]) + (rows[2] + rows[3])) + (rows[4] + rows[5])
        mean = jnp.sum(tot, axis=-1, keepdims=True) * (1.0 / D)
        cs = [r - mean for r in rows]
        sq = [c * c for c in cs]
        sq = ((sq[0] + sq[1]) + (sq[2] + sq[3])) + (sq[4] + sq[5])
        inv = lax.rsqrt(jnp.sum(sq, axis=-1, keepdims=True) * (1.0 / D) + NORM_EPS) * INV_SQRT2
        for l in range(LB):
            sn_ref[pl.ds(pl.multiple_of(n * 64, 64), 64), l * 128:(l + 1) * 128] = (cs[l] * inv).astype(jnp.bfloat16)
        return 0
    lax.fori_loop(0, 8, some_rows, 0, unroll=8)


def hidden_chunk(c, sn_ref, w1_ref, ph_ref, g):
    h = jnp.dot(sn_ref[...], w1_ref[c], preferred_element_type=jnp.float32)
    h = h + h * lax.erf(h)
    ph_ref[c, g * GROUP:(g + 1) * GROUP, :] = jnp.sum(h.reshape(64, GROUP, HC), axis=0)


def encode(groups, more_loads, x_hbm, down_hbm, taps_ref, w1_hbm, w2_hbm, ls_ref, emb_ref,
                  x_ref, down_ref, w1_ref, w2_ref, s_ref, l0_ref, l1_ref, r0_ref, r1_ref, sp_ref, sn_ref, tap_ref, x_tmp, y_tmp, ph_ref, pr_ref, sems):
    l_bufs, r_bufs = (l0_ref, l1_ref), (r0_ref, r1_ref)
    x_copy = [pltpu.make_async_copy(x_hbm.at[pl.ds(g * GROUP, GROUP)], x_ref.at[pl.ds(g * GROUP, GROUP)], sems.at[g])
              for g in range(groups)]
    down_copy = pltpu.make_async_copy(down_hbm, down_ref, sems.at[groups])
    w1_copy = [pltpu.make_async_copy(w1_hbm.at[:, pl.ds(c * HC, HC)], w1_ref.at[c], sems.at[groups + 2 + c]) for c in range(LB)]
    w2_copy = pltpu.make_async_copy(w2_hbm, w2_ref, sems.at[groups + 1])
    x_copy[0].start()
    down_copy.start()
    fill_taps(taps_ref, tap_ref)
    x_copy[0].wait()
    x_copy[1].start()
    for copy in w1_copy:
        copy.start()
    def only_norm(n, _):
        norm_rows(n, x_ref, s_ref, 0)
        return 0
    lax.fori_loop(0, GROUP * 4, only_norm, 0, unroll=8)
    make_patches(s_ref, l0_ref)
    for g in range(2, groups):
        x_copy[g].start()
    w2_copy.start()
    for copy in more_loads:
        copy.start()
    down_copy.wait()

    def norm_and_reduce(g_norm, g_red):
        per = GROUP * 4 // BSPLIT

        def step(n, _):
            if g_norm < groups:
                for k in range(per):
                    norm_rows(n * per + k, x_ref, s_ref, g_norm)
            if g_red < groups:
                reduce_rows(n, l_bufs[g_red % 2], down_ref, r_bufs[g_red % 2])
            return 0
        if g_norm < groups:
            x_copy[g_norm].wait()
        lax.fori_loop(0, BSPLIT, step, 0)
        if g_norm < groups:
            make_patches(s_ref, l_bufs[g_norm % 2])
    norm_and_reduce(1, 0)

    for g in range(groups + 1):
        if g == 1:
            for copy in w1_copy:
                copy.wait()

        def step(n, _):
            if g < groups:
                conv_lane(n, r_bufs[g % 2], tap_ref, sp_ref, pr_ref, x_tmp, y_tmp, g)
            if g >= 1:
                hidden_chunk(n, sn_ref, w1_ref, ph_ref, g - 1)
            return 0
        lax.fori_loop(0, LB, step, 0, unroll=3 if g == groups else 1)
        if g < groups:
            norm_spatial(sp_ref, sn_ref)
        if g + 1 < groups:
            norm_and_reduce(g + 2, g + 1)

    w2_copy.wait()
    br = jnp.dot(jnp.concatenate(split_bf16(jnp.concatenate([ph_ref[c] for c in range(LB)], axis=-1)), axis=0), w2_ref[...], preferred_element_type=jnp.float32)
    nt = groups * GROUP
    br = br[:nt] + br[nt:]
    pr = jnp.concatenate([pr_ref[l] for l in range(LB)], axis=-1)
    pooled = (pr + ls_ref[...].reshape(1, D) * (INV_SQRT2 * br)) * (1.0 / (HALF * HALF))
    c = pooled - jnp.mean(pooled, axis=-1, keepdims=True)
    v = jnp.mean(c * c, axis=-1, keepdims=True)
    emb_ref[...] = (c * lax.rsqrt(v + NORM_EPS)).astype(jnp.bfloat16)


HEADS = 12
HEAD_DIM = 64
SEQ_DEV = 192
HALF_SEQ = 96
CAP = 2
CODED = D + 128
FAR_NEGATIVE = -1e30
MESH = pl.DeviceIdType.MESH
PLACED = (0, 1, 3, 2)


def row_norm(values):
    center = values - jnp.sum(values, axis=-1, keepdims=True) * (1.0 / D)
    spread = jnp.sum(center * center, axis=-1, keepdims=True) * (1.0 / D)
    return center * lax.rsqrt(spread + NORM_EPS)


def greet(slides, ctxs):
    count = slides * ctxs
    me = lax.axis_index("slide") * ctxs + lax.axis_index("ctx")
    barrier = pltpu.get_barrier_semaphore()

    def one(k, _):
        peer = lax.rem(me + k, count)
        pl.semaphore_signal(barrier, inc=1, device_id=(peer // ctxs, lax.rem(peer, ctxs)), device_id_type=MESH)
        return 0
    lax.fori_loop(1, count, one, 0)


def slide_layer(slides, ctxs, loads, emb_ref, slide_ref, pos_ref, len_ref, out_ref,
                wqkv_ref, wout_ref, send_ref, recv_ref, rows_ref, k_ref, v_ref, q_ref, att_ref, peak_ref, sum_ref, acc_ref,
                a2a_send, a2a_recv, own_sem, ring_send, ring_recv):
    load_qkv, load_out = loads
    count = slides * ctxs
    tiles = emb_ref.shape[0]
    total = ctxs * SEQ_DEV
    slide = lax.axis_index("slide")
    ctx = lax.axis_index("ctx")
    me = slide * ctxs + ctx
    pos = pos_ref[...].reshape(1, tiles).astype(jnp.float32)
    block = jnp.floor((pos + 0.5) * (1.0 / SEQ_DEV))
    owner = slide_ref[...].reshape(1, tiles).astype(jnp.float32) * ctxs + block
    code = pos - block * SEQ_DEV + 1.0
    line = lax.broadcasted_iota(jnp.int32, (count * CAP, tiles), 0)
    target = (line // CAP).astype(jnp.float32)
    member = jnp.where(owner == target, 1.0, 0.0)
    before = lax.broadcasted_iota(jnp.int32, (tiles, tiles), 0) < lax.broadcasted_iota(jnp.int32, (tiles, tiles), 1)
    rank = jnp.dot(member.astype(jnp.bfloat16), jnp.where(before, 1.0, 0.0).astype(jnp.bfloat16),
                   preferred_element_type=jnp.float32)
    chosen = jnp.where(rank == (line % CAP).astype(jnp.float32), member, 0.0)
    codes = jnp.broadcast_to(jnp.sum(chosen * code, axis=1, keepdims=True), (count * CAP, 128))
    moved = jnp.dot(chosen.astype(jnp.bfloat16), emb_ref[...], preferred_element_type=jnp.float32)
    send_ref[:, :, :D] = moved.reshape(count, CAP, D).astype(jnp.bfloat16)
    send_ref[:, :, D:] = codes.reshape(count, CAP, 128).astype(jnp.bfloat16)
    pl.semaphore_wait(pltpu.get_barrier_semaphore(), count - 1)

    own = pltpu.make_async_copy(send_ref.at[me], recv_ref.at[me], own_sem)
    own.start()

    def send(k, _):
        peer = lax.rem(me + k, count)
        pltpu.make_async_remote_copy(
            src_ref=send_ref.at[peer], dst_ref=recv_ref.at[me], send_sem=a2a_send, recv_sem=a2a_recv,
            device_id=(peer // ctxs, lax.rem(peer, ctxs)), device_id_type=MESH).start()
        return 0
    lax.fori_loop(1, count, send, 0)
    own.wait()
    rest = pl.ds(0, count - 1)
    whole = pltpu.make_async_remote_copy(
        src_ref=send_ref.at[rest], dst_ref=recv_ref.at[rest], send_sem=a2a_send, recv_sem=a2a_recv,
        device_id=(slide, ctx), device_id_type=MESH)
    whole.wait_recv()

    arrived = recv_ref[...].reshape(count * CAP, CODED)
    got = arrived[:, D:].astype(jnp.float32)
    lane = lax.broadcasted_iota(jnp.int32, (count * CAP, 128), 1).astype(jnp.float32) + 1.0
    pick = jnp.concatenate([jnp.where(got == lane, 1.0, 0.0), jnp.where(got == lane + 128.0, 1.0, 0.0)], axis=1)
    mine = lax.dot_general(pick.astype(jnp.bfloat16), arrived[:, :D], (((0,), (0,)), ((), ())),
                           preferred_element_type=jnp.float32)
    rows_ref[ctx] = mine[:SEQ_DEV].astype(jnp.bfloat16)

    right = lax.rem(ctx + 1, ctxs)
    left = lax.rem(ctx + ctxs - 1, ctxs)
    first, second = pl.ds(0, HALF_SEQ), pl.ds(HALF_SEQ, HALF_SEQ)

    def hop(n, blk, half, to):
        return pltpu.make_async_remote_copy(
            src_ref=rows_ref.at[blk, half], dst_ref=rows_ref.at[blk, half],
            send_sem=ring_send.at[n], recv_sem=ring_recv.at[n], device_id=(slide, to), device_id_type=MESH)

    def keys_values(place):
        ln = row_norm(rows_ref[lax.rem(ctx + PLACED[place], ctxs)].astype(jnp.float32)).astype(jnp.bfloat16)
        at = slice(place * SEQ_DEV, (place + 1) * SEQ_DEV)
        k_ref[at, :] = jnp.dot(ln, wqkv_ref[:, D:2 * D], preferred_element_type=jnp.float32).astype(jnp.bfloat16)
        v_ref[at, :] = jnp.dot(ln, wqkv_ref[:, 2 * D:], preferred_element_type=jnp.float32).astype(jnp.bfloat16)
        return ln
    own_hops = [hop(0, ctx, first, right), hop(1, ctx, second, left), hop(2, ctx, second, right), hop(3, ctx, first, left)]
    for h in own_hops:
        h.start()
    load_qkv.wait()
    ln = keys_values(0)
    q = jnp.dot(ln, wqkv_ref[:, :D], preferred_element_type=jnp.float32)
    q_ref[...] = (q.astype(jnp.bfloat16).astype(jnp.float32) * HEAD_DIM ** (-0.5)).astype(jnp.bfloat16)
    length = len_ref[slide]
    low = lax.broadcasted_iota(jnp.int32, (SEQ_DEV, 128), 1) < HEAD_DIM

    def attend_part(place, blocks, first_part, last_part):
        size = blocks * SEQ_DEV
        lane = lax.broadcasted_iota(jnp.int32, (1, size), 1)
        key = lane + lax.rem(ctx + PLACED[place], ctxs) * SEQ_DEV
        if blocks == 2:
            key = jnp.where(lane < SEQ_DEV, key, lane + (lax.rem(ctx + PLACED[place + 1], ctxs) - 1) * SEQ_DEV)
        bias = jnp.where(key < length, 0.0, FAR_NEGATIVE)
        at = slice(place * SEQ_DEV, place * SEQ_DEV + size)
        for pair in range(HEADS // 2):
            cols = slice(pair * 128, pair * 128 + 128)
            q2 = q_ref[:, cols]
            zero = jnp.zeros_like(q2)
            both = jnp.concatenate([jnp.where(low, q2, zero), jnp.where(low, zero, q2)], axis=0)
            s = lax.dot_general(both, k_ref[at, cols], (((1,), (1,)), ((), ())), preferred_element_type=jnp.float32) + bias
            peak = jnp.max(s, axis=-1, keepdims=True)
            if not first_part:
                old = peak_ref[pair][:, :1]
                peak = jnp.maximum(peak, old)
                scale = jnp.exp(old - peak)
            w = jnp.exp(s - peak)
            denom = jnp.sum(w, axis=-1, keepdims=True)
            o = jnp.dot(w.astype(jnp.bfloat16), v_ref[at, cols], preferred_element_type=jnp.float32)
            if not first_part:
                denom = denom + sum_ref[pair][:, :1] * scale
                o = o + acc_ref[pair] * scale
            if last_part:
                o = o / denom
                att_ref[:, cols] = jnp.where(low, o[:SEQ_DEV], o[SEQ_DEV:]).astype(jnp.bfloat16)
            else:
                peak_ref[pair] = jnp.broadcast_to(peak, (2 * SEQ_DEV, 128))
                sum_ref[pair] = jnp.broadcast_to(denom, (2 * SEQ_DEV, 128))
                acc_ref[pair] = o

    own_hops[0].wait_recv()
    onward = hop(4, left, first, right)
    onward.start()
    own_hops[1].wait_recv()
    back = hop(5, right, second, left)
    back.start()
    attend_part(0, 1, True, False)
    own_hops[2].wait_recv()
    own_hops[3].wait_recv()
    keys_values(1)
    keys_values(2)
    attend_part(1, 2, False, False)
    onward.wait_recv()
    back.wait_recv()
    keys_values(3)
    attend_part(3, 1, False, True)
    for h in own_hops + [onward, back]:
        h.wait_send()
    whole.wait_send()
    load_out.wait()
    out = jnp.dot(att_ref[...], wout_ref[...], preferred_element_type=jnp.float32)
    out = out + rows_ref[ctx].astype(jnp.float32)
    row = lax.broadcasted_iota(jnp.int32, (SEQ_DEV, 1), 0) + ctx * SEQ_DEV
    out_ref[...] = jnp.where(row < length, out, 0.0).astype(jnp.bfloat16)


def whole_kernel(groups, slides, ctxs, x_hbm, down_hbm, taps_ref, w1_hbm, w2_hbm, ls_ref, wqkv_hbm, wout_hbm,
                 slide_ref, pos_ref, len_ref, out_ref, emb_ref, load_sem, wqkv_ref, wout_ref, send_ref, recv_ref, rows_ref,
                 k_ref, v_ref, q_ref, att_ref, peak_ref, sum_ref, acc_ref, a2a_send, a2a_recv, own_sem, ring_send, ring_recv, *encoder_refs):
    greet(slides, ctxs)
    loads = (pltpu.make_async_copy(wqkv_hbm, wqkv_ref, load_sem.at[0]), pltpu.make_async_copy(wout_hbm, wout_ref, load_sem.at[1]))
    encode(groups, loads, x_hbm, down_hbm, taps_ref, w1_hbm, w2_hbm, ls_ref, emb_ref, *encoder_refs)
    slide_layer(slides, ctxs, loads, emb_ref, slide_ref, pos_ref, len_ref, out_ref,
                wqkv_ref, wout_ref, send_ref, recv_ref, rows_ref, k_ref, v_ref, q_ref, att_ref, peak_ref, sum_ref, acc_ref,
                a2a_send, a2a_recv, own_sem, ring_send, ring_recv)


def shards(x, down, taps, w1, w2, ls, qkv_weight, out_weight, tile_slide, tile_pos, slide_len):
    slides, ctxs = lax.axis_size("slide"), lax.axis_size("ctx")
    nt = x.shape[0]
    groups = nt // GROUP
    count = slides * ctxs
    total = ctxs * SEQ_DEV
    hbm = pl.BlockSpec(memory_space=pl.ANY)
    vmem = pl.BlockSpec(memory_space=pltpu.VMEM)
    return pl.pallas_call(
        functools.partial(whole_kernel, groups, slides, ctxs),
        out_shape=jax.ShapeDtypeStruct((SEQ_DEV, D), jnp.bfloat16),
        in_specs=[hbm, hbm, vmem, hbm, hbm, vmem, hbm, hbm, vmem, vmem, pl.BlockSpec(memory_space=pltpu.SMEM)],
        out_specs=vmem,
        scratch_shapes=[
            pltpu.VMEM((nt, D), jnp.bfloat16), pltpu.SemaphoreType.DMA((2,)),
            pltpu.VMEM((D, 3 * D), jnp.bfloat16), pltpu.VMEM((D, D), jnp.bfloat16),
            pltpu.VMEM((count, CAP, CODED), jnp.bfloat16), pltpu.VMEM((count, CAP, CODED), jnp.bfloat16),
            pltpu.VMEM((ctxs, SEQ_DEV, D), jnp.bfloat16),
            pltpu.VMEM((total, D), jnp.bfloat16), pltpu.VMEM((total, D), jnp.bfloat16),
            pltpu.VMEM((SEQ_DEV, D), jnp.bfloat16), pltpu.VMEM((SEQ_DEV, D), jnp.bfloat16),
            pltpu.VMEM((HEADS // 2, 2 * SEQ_DEV, 128), jnp.float32), pltpu.VMEM((HEADS // 2, 2 * SEQ_DEV, 128), jnp.float32),
            pltpu.VMEM((HEADS // 2, 2 * SEQ_DEV, 128), jnp.float32),
            pltpu.SemaphoreType.DMA, pltpu.SemaphoreType.DMA, pltpu.SemaphoreType.DMA,
            pltpu.SemaphoreType.DMA((6,)), pltpu.SemaphoreType.DMA((6,)),
            pltpu.VMEM((nt, 16, 16, C_IN), jnp.bfloat16),
            pltpu.VMEM((4 * C_IN, D), jnp.bfloat16),
            pltpu.VMEM((LB, D, HC), jnp.bfloat16),
            pltpu.VMEM((MLP, D), jnp.bfloat16),
            pltpu.VMEM((3, GROUP * PITCH, 128), jnp.float32),
            pltpu.VMEM((64 * GROUP, 4 * C_IN), jnp.bfloat16),
            pltpu.VMEM((64 * GROUP, 4 * C_IN), jnp.bfloat16),
            pltpu.VMEM((LB, 64, GROUP, 128), jnp.float32),
            pltpu.VMEM((LB, 64, GROUP, 128), jnp.float32),
            pltpu.VMEM((LB, 64, GROUP, 128), jnp.float32),
            pltpu.VMEM((64 * GROUP, D), jnp.bfloat16),
            pltpu.VMEM((LB, len(TAP_SUMS), 8, 128), jnp.float32),
            pltpu.VMEM((12, 3, 4, GROUP, 128), jnp.float32),
            pltpu.VMEM((13, HALF, GROUP, 128), jnp.float32),
            pltpu.VMEM((LB, nt, HC), jnp.float32),
            pltpu.VMEM((LB, nt, 128), jnp.float32),
            pltpu.SemaphoreType.DMA((groups + 2 + LB,)),
        ],
        compiler_params=pltpu.CompilerParams(collective_id=0, has_side_effects=True, vmem_limit_bytes=50 << 20),
        name="whole",
    )(x, down, taps, w1, w2, ls, qkv_weight[0], out_weight[0], tile_slide, tile_pos, slide_len)


def solution(mesh):
    whole = P(("slide", "ctx"))
    return jax.shard_map(
        shards,
        mesh=mesh,
        in_specs=(whole, P(), P(), P(), P(), P(), P(), P(), whole, whole, P()),
        out_specs=whole,
        check_vma=False,
    )
```

```python
import functools

import jax
import jax.numpy as jnp
from jax import lax
from jax.experimental import pallas as pl
from jax.experimental.pallas import tpu as pltpu
from jax.sharding import PartitionSpec as P

NORM_EPS = 1e-06
GROUP = 8
HALF = 8
KS = 7
C_IN = 384
D = 768
LB = D // 128
MLP = 3072
HC = 512
PITCH = 257
INV_SQRT2 = 0.7071067811865476
BSPLIT = 2


def split_bf16(values):
    high = values.astype(jnp.bfloat16)
    return high, (values - high.astype(jnp.float32)).astype(jnp.bfloat16)


def norm_rows(n, x_ref, s_ref, g):
    t = n // 4
    y = (n % 4) * 4
    x = x_ref[g * GROUP + t, pl.ds(y, 4)].reshape(64, C_IN).astype(jnp.float32)
    c = x - jnp.sum(x, axis=-1, keepdims=True) * (1.0 / C_IN)
    v = jnp.sum(c * c, axis=-1, keepdims=True) * (1.0 / C_IN)
    o = c * lax.rsqrt(v + NORM_EPS)
    for l in range(3):
        s_ref[l, pl.ds(t * PITCH + y * 16, 64), :] = o[:, l * 128:(l + 1) * 128]


def make_patches(s_ref, l_ref):
    def patch_rows(n, _):
        i = n // 4
        jp = (n % 4) * 2
        row = pl.multiple_of((i * HALF + jp) * GROUP, 16)
        for dy in range(2):
            for dx in range(2):
                for l in range(3):
                    pos = (2 * i + dy) * 16 + 2 * jp + dx
                    a = s_ref[l, pl.ds(pos, GROUP, stride=PITCH), :]
                    b = s_ref[l, pl.ds(pos + 2, GROUP, stride=PITCH), :]
                    col = (dy * 2 + dx) * C_IN + l * 128
                    l_ref[pl.ds(row, 16), col:col + 128] = jnp.concatenate([a, b], axis=0).astype(jnp.bfloat16)
        return 0
    lax.fori_loop(0, HALF * HALF // 2, patch_rows, 0, unroll=2)


def reduce_rows(m, l_ref, down_ref, r_ref):
    rows = 64 * GROUP // BSPLIT
    lhs = l_ref[pl.ds(pl.multiple_of(m * rows, rows), rows), :]
    red = jnp.dot(lhs, down_ref[...], preferred_element_type=jnp.float32)
    red = red.astype(jnp.bfloat16).astype(jnp.float32)
    for h in range(LB):
        r_ref[h, pl.ds(m * (rows // GROUP), rows // GROUP)] = red[:, h * 128:(h + 1) * 128].reshape(rows // GROUP, GROUP, 128)


def tap_axis(part):
    odd = {k: (2 * k + 3,) for k in (-1, 0, 1)}
    even = {k: (2 * k + 2,) for k in (-1, 0, 1, 2)}
    if part == 0:
        return odd
    if part == 1:
        return even
    return {k: even[k] + odd.get(k, ()) for k in even}


TAP_SUMS = []
TAP_AT = {}
for _p in range(3):
    for _q in range(3):
        for _k, _ra in tap_axis(_p).items():
            for _l, _cb in tap_axis(_q).items():
                TAP_AT[(_p, _q, _k, _l)] = len(TAP_SUMS)
                TAP_SUMS.append([a * KS + b for a in _ra for b in _cb])


def fill_taps(taps_ref, tap_ref):
    t = taps_ref[...].astype(jnp.float32)
    for n, sums in enumerate(TAP_SUMS):
        row = t[sums[0]:sums[0] + 1]
        for k in sums[1:]:
            row = row + t[k:k + 1]
        for l in range(LB):
            tap_ref[l, n] = jnp.broadcast_to(row[:, l * 128:(l + 1) * 128], (8, 128))


def conv_lane(l, r_ref, tap_ref, sp_ref, pr_ref, x_tmp, y_tmp, g):
    spots = range(4)
    psum = None
    for i in range(HALF):
        xs = [r_ref[l, i * HALF + j] for j in range(HALF)]
        for j in spots:
            x_tmp[i, 2, j] = xs[2 * j] + xs[2 * j + 1]
    for i in spots:
        row = None
        for q in range(3):
            for j in spots:
                top = r_ref[l, 2 * i * HALF + 2 * j + q] if q < 2 else x_tmp[2 * i, 2, j]
                low = r_ref[l, (2 * i + 1) * HALF + 2 * j + q] if q < 2 else x_tmp[2 * i + 1, 2, j]
                both = top + low
                x_tmp[8 + i, q, j] = both
                if q == 2:
                    row = both if row is None else row + both
        psum = row if psum is None else psum + row
    pr_ref[l, g * GROUP:(g + 1) * GROUP, :] = psum

    def load(p, q, i, j):
        if p == 2:
            return x_tmp[8 + i, q, j]
        if q == 2:
            return x_tmp[2 * i + p, 2, j]
        return r_ref[l, (2 * i + p) * HALF + 2 * j + q]

    outs = [range(4), range(-1, 4), range(4)]
    base = [0, 5, 9]
    for p in range(3):
        for i in outs[p]:
            part = []
            for q in range(3):
                acc = {}
                for k in tap_axis(p):
                    if not 0 <= i + k < 4:
                        continue
                    xs = [load(p, q, i + k, j) for j in spots]
                    for m in tap_axis(q):
                        w = tap_ref[l, TAP_AT[(p, q, k, m)]]
                        for j in outs[q]:
                            if 0 <= j + m < 4:
                                term = xs[j + m] * w
                                acc[j] = acc[j] + term if j in acc else term
                part.append(acc)
            for j in spots:
                y_tmp[base[p] + i, 2 * j] = part[0][j] + part[1][j - 1]
                y_tmp[base[p] + i, 2 * j + 1] = part[2][j] - part[0][j] - part[1][j]
    for i in spots:
        for j in range(HALF):
            a, b, before, c = y_tmp[i, j], y_tmp[5 + i, j], y_tmp[4 + i, j], y_tmp[9 + i, j]
            sp_ref[l, 2 * i * HALF + j] = a + before
            sp_ref[l, (2 * i + 1) * HALF + j] = c - a - b


def norm_spatial(sp_ref, sn_ref):
    def some_rows(n, _):
        rows = [sp_ref[l, pl.ds(n * 8, 8)].reshape(64, 128) for l in range(LB)]
        tot = ((rows[0] + rows[1]) + (rows[2] + rows[3])) + (rows[4] + rows[5])
        mean = jnp.sum(tot, axis=-1, keepdims=True) * (1.0 / D)
        cs = [r - mean for r in rows]
        sq = [c * c for c in cs]
        sq = ((sq[0] + sq[1]) + (sq[2] + sq[3])) + (sq[4] + sq[5])
        inv = lax.rsqrt(jnp.sum(sq, axis=-1, keepdims=True) * (1.0 / D) + NORM_EPS) * INV_SQRT2
        for l in range(LB):
            sn_ref[pl.ds(pl.multiple_of(n * 64, 64), 64), l * 128:(l + 1) * 128] = (cs[l] * inv).astype(jnp.bfloat16)
        return 0
    lax.fori_loop(0, 8, some_rows, 0, unroll=8)


def hidden_chunk(c, sn_ref, w1_ref, ph_ref, g):
    h = jnp.dot(sn_ref[...], w1_ref[c], preferred_element_type=jnp.float32)
    h = h + h * lax.erf(h)
    ph_ref[c, g * GROUP:(g + 1) * GROUP, :] = jnp.sum(h.reshape(64, GROUP, HC), axis=0)


def encode(groups, more_loads, x_hbm, down_hbm, taps_ref, w1_hbm, w2_hbm, ls_ref, emb_ref,
                  x_ref, down_ref, w1_ref, w2_ref, s_ref, l0_ref, l1_ref, r0_ref, r1_ref, sp_ref, sn_ref, tap_ref, x_tmp, y_tmp, ph_ref, pr_ref, sems):
    l_bufs, r_bufs = (l0_ref, l1_ref), (r0_ref, r1_ref)
    x_copy = [pltpu.make_async_copy(x_hbm.at[pl.ds(g * GROUP, GROUP)], x_ref.at[pl.ds(g * GROUP, GROUP)], sems.at[g])
              for g in range(groups)]
    down_copy = pltpu.make_async_copy(down_hbm, down_ref, sems.at[groups])
    w1_copy = [pltpu.make_async_copy(w1_hbm.at[:, pl.ds(c * HC, HC)], w1_ref.at[c], sems.at[groups + 2 + c]) for c in range(LB)]
    w2_copy = pltpu.make_async_copy(w2_hbm, w2_ref, sems.at[groups + 1])
    x_copy[0].start()
    down_copy.start()
    fill_taps(taps_ref, tap_ref)
    x_copy[0].wait()
    x_copy[1].start()
    for copy in w1_copy:
        copy.start()
    def only_norm(n, _):
        norm_rows(n, x_ref, s_ref, 0)
        return 0
    lax.fori_loop(0, GROUP * 4, only_norm, 0, unroll=8)
    make_patches(s_ref, l0_ref)
    for g in range(2, groups):
        x_copy[g].start()
    w2_copy.start()
    for copy in more_loads:
        copy.start()
    down_copy.wait()

    def norm_and_reduce(g_norm, g_red):
        per = GROUP * 4 // BSPLIT

        def step(n, _):
            if g_norm < groups:
                for k in range(per):
                    norm_rows(n * per + k, x_ref, s_ref, g_norm)
            if g_red < groups:
                reduce_rows(n, l_bufs[g_red % 2], down_ref, r_bufs[g_red % 2])
            return 0
        if g_norm < groups:
            x_copy[g_norm].wait()
        lax.fori_loop(0, BSPLIT, step, 0)
        if g_norm < groups:
            make_patches(s_ref, l_bufs[g_norm % 2])
    norm_and_reduce(1, 0)

    for g in range(groups + 1):
        if g == 1:
            for copy in w1_copy:
                copy.wait()

        def step(n, _):
            if g < groups:
                conv_lane(n, r_bufs[g % 2], tap_ref, sp_ref, pr_ref, x_tmp, y_tmp, g)
            if g >= 1:
                hidden_chunk(n, sn_ref, w1_ref, ph_ref, g - 1)
            return 0
        lax.fori_loop(0, LB, step, 0, unroll=3 if g == groups else 1)
        if g < groups:
            norm_spatial(sp_ref, sn_ref)
        if g + 1 < groups:
            norm_and_reduce(g + 2, g + 1)

    w2_copy.wait()
    br = jnp.dot(jnp.concatenate(split_bf16(jnp.concatenate([ph_ref[c] for c in range(LB)], axis=-1)), axis=0), w2_ref[...], preferred_element_type=jnp.float32)
    nt = groups * GROUP
    br = br[:nt] + br[nt:]
    pr = jnp.concatenate([pr_ref[l] for l in range(LB)], axis=-1)
    pooled = (pr + ls_ref[...].reshape(1, D) * (INV_SQRT2 * br)) * (1.0 / (HALF * HALF))
    c = pooled - jnp.mean(pooled, axis=-1, keepdims=True)
    v = jnp.mean(c * c, axis=-1, keepdims=True)
    emb_ref[...] = (c * lax.rsqrt(v + NORM_EPS)).astype(jnp.bfloat16)


HEADS = 12
HEAD_DIM = 64
SEQ_DEV = 192
HALF_SEQ = 96
CAP = 2
CODED = D + 128
FAR_NEGATIVE = -1e30
MESH = pl.DeviceIdType.MESH


def row_norm(values):
    center = values - jnp.sum(values, axis=-1, keepdims=True) * (1.0 / D)
    spread = jnp.sum(center * center, axis=-1, keepdims=True) * (1.0 / D)
    return center * lax.rsqrt(spread + NORM_EPS)


def greet(slides, ctxs):
    count = slides * ctxs
    me = lax.axis_index("slide") * ctxs + lax.axis_index("ctx")
    barrier = pltpu.get_barrier_semaphore()

    def one(k, _):
        peer = lax.rem(me + k, count)
        pl.semaphore_signal(barrier, inc=1, device_id=(peer // ctxs, lax.rem(peer, ctxs)), device_id_type=MESH)
        return 0
    lax.fori_loop(1, count, one, 0)


def slide_layer(slides, ctxs, loads, emb_ref, slide_ref, pos_ref, len_ref, out_ref,
                wqkv_ref, wout_ref, send_ref, recv_ref, rows_ref, k_ref, v_ref, q_ref, att_ref,
                a2a_send, a2a_recv, own_sem, ring_send, ring_recv):
    load_qkv, load_out = loads
    count = slides * ctxs
    tiles = emb_ref.shape[0]
    total = ctxs * SEQ_DEV
    slide = lax.axis_index("slide")
    ctx = lax.axis_index("ctx")
    me = slide * ctxs + ctx
    pos = pos_ref[...].reshape(1, tiles).astype(jnp.float32)
    block = jnp.floor((pos + 0.5) * (1.0 / SEQ_DEV))
    owner = slide_ref[...].reshape(1, tiles).astype(jnp.float32) * ctxs + block
    code = pos - block * SEQ_DEV + 1.0
    line = lax.broadcasted_iota(jnp.int32, (count * CAP, tiles), 0)
    target = (line // CAP).astype(jnp.float32)
    member = jnp.where(owner == target, 1.0, 0.0)
    before = lax.broadcasted_iota(jnp.int32, (tiles, tiles), 0) < lax.broadcasted_iota(jnp.int32, (tiles, tiles), 1)
    rank = jnp.dot(member.astype(jnp.bfloat16), jnp.where(before, 1.0, 0.0).astype(jnp.bfloat16),
                   preferred_element_type=jnp.float32)
    chosen = jnp.where(rank == (line % CAP).astype(jnp.float32), member, 0.0)
    codes = jnp.broadcast_to(jnp.sum(chosen * code, axis=1, keepdims=True), (count * CAP, 128))
    moved = jnp.dot(chosen.astype(jnp.bfloat16), emb_ref[...], preferred_element_type=jnp.float32)
    send_ref[:, :, :D] = moved.reshape(count, CAP, D).astype(jnp.bfloat16)
    send_ref[:, :, D:] = codes.reshape(count, CAP, 128).astype(jnp.bfloat16)
    pl.semaphore_wait(pltpu.get_barrier_semaphore(), count - 1)

    own = pltpu.make_async_copy(send_ref.at[me], recv_ref.at[me], own_sem)
    own.start()

    def send(k, _):
        peer = lax.rem(me + k, count)
        pltpu.make_async_remote_copy(
            src_ref=send_ref.at[peer], dst_ref=recv_ref.at[me], send_sem=a2a_send, recv_sem=a2a_recv,
            device_id=(peer // ctxs, lax.rem(peer, ctxs)), device_id_type=MESH).start()
        return 0
    lax.fori_loop(1, count, send, 0)
    own.wait()
    rest = pl.ds(0, count - 1)
    whole = pltpu.make_async_remote_copy(
        src_ref=send_ref.at[rest], dst_ref=recv_ref.at[rest], send_sem=a2a_send, recv_sem=a2a_recv,
        device_id=(slide, ctx), device_id_type=MESH)
    whole.wait_recv()

    arrived = recv_ref[...].reshape(count * CAP, CODED)
    got = arrived[:, D:].astype(jnp.float32)
    lane = lax.broadcasted_iota(jnp.int32, (count * CAP, 128), 1).astype(jnp.float32) + 1.0
    pick = jnp.concatenate([jnp.where(got == lane, 1.0, 0.0), jnp.where(got == lane + 128.0, 1.0, 0.0)], axis=1)
    mine = lax.dot_general(pick.astype(jnp.bfloat16), arrived[:, :D], (((0,), (0,)), ((), ())),
                           preferred_element_type=jnp.float32)
    rows_ref[ctx] = mine[:SEQ_DEV].astype(jnp.bfloat16)

    right = lax.rem(ctx + 1, ctxs)
    left = lax.rem(ctx + ctxs - 1, ctxs)
    far = lax.rem(ctx + 2, ctxs)
    first, second = pl.ds(0, HALF_SEQ), pl.ds(HALF_SEQ, HALF_SEQ)

    def hop(n, blk, half, to):
        return pltpu.make_async_remote_copy(
            src_ref=rows_ref.at[blk, half], dst_ref=rows_ref.at[blk, half],
            send_sem=ring_send.at[n], recv_sem=ring_recv.at[n], device_id=(slide, to), device_id_type=MESH)

    def keys_values(blk):
        ln = row_norm(rows_ref[blk].astype(jnp.float32)).astype(jnp.bfloat16)
        at = pl.ds(pl.multiple_of(blk * SEQ_DEV, 64), SEQ_DEV)
        k_ref[at, :] = jnp.dot(ln, wqkv_ref[:, D:2 * D], preferred_element_type=jnp.float32).astype(jnp.bfloat16)
        v_ref[at, :] = jnp.dot(ln, wqkv_ref[:, 2 * D:], preferred_element_type=jnp.float32).astype(jnp.bfloat16)
        return ln
    own_hops = [hop(0, ctx, first, right), hop(1, ctx, second, left), hop(2, ctx, second, right), hop(3, ctx, first, left)]
    for h in own_hops:
        h.start()
    load_qkv.wait()
    ln = keys_values(ctx)
    q = jnp.dot(ln, wqkv_ref[:, :D], preferred_element_type=jnp.float32)
    q_ref[...] = (q.astype(jnp.bfloat16).astype(jnp.float32) * HEAD_DIM ** (-0.5)).astype(jnp.bfloat16)
    own_hops[0].wait_recv()
    onward = hop(4, left, first, right)
    onward.start()
    own_hops[1].wait_recv()
    back = hop(5, right, second, left)
    back.start()
    own_hops[2].wait_recv()
    own_hops[3].wait_recv()

    def near(n, _):
        keys_values(lax.rem(ctx + 1 + 2 * n, ctxs))
        return 0
    lax.fori_loop(0, 2, near, 0)
    onward.wait_recv()
    back.wait_recv()
    keys_values(far)
    for h in own_hops + [onward, back]:
        h.wait_send()
    whole.wait_send()
    load_out.wait()

    length = len_ref[slide]
    key = lax.broadcasted_iota(jnp.int32, (1, total), 1)
    bias = jnp.where(key < length, 0.0, FAR_NEGATIVE)
    low = lax.broadcasted_iota(jnp.int32, (SEQ_DEV, 128), 1) < HEAD_DIM
    for pair in range(HEADS // 2):
        cols = slice(pair * 128, pair * 128 + 128)
        q2 = q_ref[:, cols]
        zero = jnp.zeros_like(q2)
        both = jnp.concatenate([jnp.where(low, q2, zero), jnp.where(low, zero, q2)], axis=0)
        s = lax.dot_general(both, k_ref[:, cols], (((1,), (1,)), ((), ())), preferred_element_type=jnp.float32) + bias
        w = jnp.exp(s - jnp.max(s, axis=-1, keepdims=True))
        denom = jnp.sum(w, axis=-1, keepdims=True)
        o = jnp.dot(w.astype(jnp.bfloat16), v_ref[:, cols], preferred_element_type=jnp.float32) * (1.0 / denom)
        att_ref[:, cols] = jnp.where(low, o[:SEQ_DEV], o[SEQ_DEV:]).astype(jnp.bfloat16)
    out = jnp.dot(att_ref[...], wout_ref[...], preferred_element_type=jnp.float32)
    out = out + rows_ref[ctx].astype(jnp.float32)
    row = lax.broadcasted_iota(jnp.int32, (SEQ_DEV, 1), 0) + ctx * SEQ_DEV
    out_ref[...] = jnp.where(row < length, out, 0.0).astype(jnp.bfloat16)


def whole_kernel(groups, slides, ctxs, x_hbm, down_hbm, taps_ref, w1_hbm, w2_hbm, ls_ref, wqkv_hbm, wout_hbm,
                 slide_ref, pos_ref, len_ref, out_ref, emb_ref, load_sem, wqkv_ref, wout_ref, send_ref, recv_ref, rows_ref,
                 k_ref, v_ref, q_ref, att_ref, a2a_send, a2a_recv, own_sem, ring_send, ring_recv, *encoder_refs):
    greet(slides, ctxs)
    loads = (pltpu.make_async_copy(wqkv_hbm, wqkv_ref, load_sem.at[0]), pltpu.make_async_copy(wout_hbm, wout_ref, load_sem.at[1]))
    encode(groups, loads, x_hbm, down_hbm, taps_ref, w1_hbm, w2_hbm, ls_ref, emb_ref, *encoder_refs)
    slide_layer(slides, ctxs, loads, emb_ref, slide_ref, pos_ref, len_ref, out_ref,
                wqkv_ref, wout_ref, send_ref, recv_ref, rows_ref, k_ref, v_ref, q_ref, att_ref,
                a2a_send, a2a_recv, own_sem, ring_send, ring_recv)


def shards(x, down, taps, w1, w2, ls, qkv_weight, out_weight, tile_slide, tile_pos, slide_len):
    slides, ctxs = lax.axis_size("slide"), lax.axis_size("ctx")
    nt = x.shape[0]
    groups = nt // GROUP
    count = slides * ctxs
    total = ctxs * SEQ_DEV
    hbm = pl.BlockSpec(memory_space=pl.ANY)
    vmem = pl.BlockSpec(memory_space=pltpu.VMEM)
    return pl.pallas_call(
        functools.partial(whole_kernel, groups, slides, ctxs),
        out_shape=jax.ShapeDtypeStruct((SEQ_DEV, D), jnp.bfloat16),
        in_specs=[hbm, hbm, vmem, hbm, hbm, vmem, hbm, hbm, vmem, vmem, pl.BlockSpec(memory_space=pltpu.SMEM)],
        out_specs=vmem,
        scratch_shapes=[
            pltpu.VMEM((nt, D), jnp.bfloat16), pltpu.SemaphoreType.DMA((2,)),
            pltpu.VMEM((D, 3 * D), jnp.bfloat16), pltpu.VMEM((D, D), jnp.bfloat16),
            pltpu.VMEM((count, CAP, CODED), jnp.bfloat16), pltpu.VMEM((count, CAP, CODED), jnp.bfloat16),
            pltpu.VMEM((ctxs, SEQ_DEV, D), jnp.bfloat16),
            pltpu.VMEM((total, D), jnp.bfloat16), pltpu.VMEM((total, D), jnp.bfloat16),
            pltpu.VMEM((SEQ_DEV, D), jnp.bfloat16), pltpu.VMEM((SEQ_DEV, D), jnp.bfloat16),
            pltpu.SemaphoreType.DMA, pltpu.SemaphoreType.DMA, pltpu.SemaphoreType.DMA,
            pltpu.SemaphoreType.DMA((6,)), pltpu.SemaphoreType.DMA((6,)),
            pltpu.VMEM((nt, 16, 16, C_IN), jnp.bfloat16),
            pltpu.VMEM((4 * C_IN, D), jnp.bfloat16),
            pltpu.VMEM((LB, D, HC), jnp.bfloat16),
            pltpu.VMEM((MLP, D), jnp.bfloat16),
            pltpu.VMEM((3, GROUP * PITCH, 128), jnp.float32),
            pltpu.VMEM((64 * GROUP, 4 * C_IN), jnp.bfloat16),
            pltpu.VMEM((64 * GROUP, 4 * C_IN), jnp.bfloat16),
            pltpu.VMEM((LB, 64, GROUP, 128), jnp.float32),
            pltpu.VMEM((LB, 64, GROUP, 128), jnp.float32),
            pltpu.VMEM((LB, 64, GROUP, 128), jnp.float32),
            pltpu.VMEM((64 * GROUP, D), jnp.bfloat16),
            pltpu.VMEM((LB, len(TAP_SUMS), 8, 128), jnp.float32),
            pltpu.VMEM((12, 3, 4, GROUP, 128), jnp.float32),
            pltpu.VMEM((13, HALF, GROUP, 128), jnp.float32),
            pltpu.VMEM((LB, nt, HC), jnp.float32),
            pltpu.VMEM((LB, nt, 128), jnp.float32),
            pltpu.SemaphoreType.DMA((groups + 2 + LB,)),
        ],
        compiler_params=pltpu.CompilerParams(collective_id=0, has_side_effects=True, vmem_limit_bytes=60 << 20),
        name="whole",
    )(x, down, taps, w1, w2, ls, qkv_weight[0], out_weight[0], tile_slide, tile_pos, slide_len)


def solution(mesh):
    whole = P(("slide", "ctx"))
    return jax.shard_map(
        shards,
        mesh=mesh,
        in_specs=(whole, P(), P(), P(), P(), P(), P(), P(), whole, whole, P()),
        out_specs=whole,
        check_vma=False,
    )
```

```python
import functools

import jax
import jax.numpy as jnp
from jax import lax
from jax.experimental import pallas as pl
from jax.experimental.pallas import tpu as pltpu
from jax.sharding import PartitionSpec as P

NORM_EPS = 1e-06
GROUP = 8
HALF = 8
KS = 7
C_IN = 384
D = 768
LB = D // 128
MLP = 3072
HC = 512
PITCH = 257
INV_SQRT2 = 0.7071067811865476
BSPLIT = 2


def split_bf16(values):
    high = values.astype(jnp.bfloat16)
    return high, (values - high.astype(jnp.float32)).astype(jnp.bfloat16)


def norm_rows(n, x_ref, s_ref, g):
    t = n // 4
    y = (n % 4) * 4
    x = x_ref[g * GROUP + t, pl.ds(y, 4)].reshape(64, C_IN).astype(jnp.float32)
    c = x - jnp.sum(x, axis=-1, keepdims=True) * (1.0 / C_IN)
    v = jnp.sum(c * c, axis=-1, keepdims=True) * (1.0 / C_IN)
    o = c * lax.rsqrt(v + NORM_EPS)
    for l in range(3):
        s_ref[l, pl.ds(t * PITCH + y * 16, 64), :] = o[:, l * 128:(l + 1) * 128]


def make_patches(s_ref, l_ref):
    def patch_rows(n, _):
        i = n // 4
        jp = (n % 4) * 2
        row = pl.multiple_of((i * HALF + jp) * GROUP, 16)
        for dy in range(2):
            for dx in range(2):
                for l in range(3):
                    pos = (2 * i + dy) * 16 + 2 * jp + dx
                    a = s_ref[l, pl.ds(pos, GROUP, stride=PITCH), :]
                    b = s_ref[l, pl.ds(pos + 2, GROUP, stride=PITCH), :]
                    col = (dy * 2 + dx) * C_IN + l * 128
                    l_ref[pl.ds(row, 16), col:col + 128] = jnp.concatenate([a, b], axis=0).astype(jnp.bfloat16)
        return 0
    lax.fori_loop(0, HALF * HALF // 2, patch_rows, 0, unroll=2)


def reduce_rows(m, l_ref, down_ref, r_ref):
    rows = 64 * GROUP // BSPLIT
    lhs = l_ref[pl.ds(pl.multiple_of(m * rows, rows), rows), :]
    red = jnp.dot(lhs, down_ref[...], preferred_element_type=jnp.float32)
    red = red.astype(jnp.bfloat16).astype(jnp.float32)
    for h in range(LB):
        r_ref[h, pl.ds(m * (rows // GROUP), rows // GROUP)] = red[:, h * 128:(h + 1) * 128].reshape(rows // GROUP, GROUP, 128)


def tap_axis(part):
    odd = {k: (2 * k + 3,) for k in (-1, 0, 1)}
    even = {k: (2 * k + 2,) for k in (-1, 0, 1, 2)}
    if part == 0:
        return odd
    if part == 1:
        return even
    return {k: even[k] + odd.get(k, ()) for k in even}


TAP_SUMS = []
TAP_AT = {}
for _p in range(3):
    for _q in range(3):
        for _k, _ra in tap_axis(_p).items():
            for _l, _cb in tap_axis(_q).items():
                TAP_AT[(_p, _q, _k, _l)] = len(TAP_SUMS)
                TAP_SUMS.append([a * KS + b for a in _ra for b in _cb])


def fill_taps(taps_ref, tap_ref):
    t = taps_ref[...].astype(jnp.float32)
    for n, sums in enumerate(TAP_SUMS):
        row = t[sums[0]:sums[0] + 1]
        for k in sums[1:]:
            row = row + t[k:k + 1]
        for l in range(LB):
            tap_ref[l, n] = jnp.broadcast_to(row[:, l * 128:(l + 1) * 128], (8, 128))


def conv_lane(l, r_ref, tap_ref, sp_ref, pr_ref, x_tmp, y_tmp, g):
    spots = range(4)
    psum = None
    for i in range(HALF):
        xs = [r_ref[l, i * HALF + j] for j in range(HALF)]
        for j in spots:
            x_tmp[i, 2, j] = xs[2 * j] + xs[2 * j + 1]
    for i in spots:
        row = None
        for q in range(3):
            for j in spots:
                top = r_ref[l, 2 * i * HALF + 2 * j + q] if q < 2 else x_tmp[2 * i, 2, j]
                low = r_ref[l, (2 * i + 1) * HALF + 2 * j + q] if q < 2 else x_tmp[2 * i + 1, 2, j]
                both = top + low
                x_tmp[8 + i, q, j] = both
                if q == 2:
                    row = both if row is None else row + both
        psum = row if psum is None else psum + row
    pr_ref[l, g * GROUP:(g + 1) * GROUP, :] = psum

    def load(p, q, i, j):
        if p == 2:
            return x_tmp[8 + i, q, j]
        if q == 2:
            return x_tmp[2 * i + p, 2, j]
        return r_ref[l, (2 * i + p) * HALF + 2 * j + q]

    outs = [range(4), range(-1, 4), range(4)]
    base = [0, 5, 9]
    for p in range(3):
        for i in outs[p]:
            part = []
            for q in range(3):
                acc = {}
                for k in tap_axis(p):
                    if not 0 <= i + k < 4:
                        continue
                    xs = [load(p, q, i + k, j) for j in spots]
                    for m in tap_axis(q):
                        w = tap_ref[l, TAP_AT[(p, q, k, m)]]
                        for j in outs[q]:
                            if 0 <= j + m < 4:
                                term = xs[j + m] * w
                                acc[j] = acc[j] + term if j in acc else term
                part.append(acc)
            for j in spots:
                y_tmp[base[p] + i, 2 * j] = part[0][j] + part[1][j - 1]
                y_tmp[base[p] + i, 2 * j + 1] = part[2][j] - part[0][j] - part[1][j]
    for i in spots:
        for j in range(HALF):
            a, b, before, c = y_tmp[i, j], y_tmp[5 + i, j], y_tmp[4 + i, j], y_tmp[9 + i, j]
            sp_ref[l, 2 * i * HALF + j] = a + before
            sp_ref[l, (2 * i + 1) * HALF + j] = c - a - b


def norm_spatial(sp_ref, sn_ref):
    def some_rows(n, _):
        rows = [sp_ref[l, pl.ds(n * 8, 8)].reshape(64, 128) for l in range(LB)]
        tot = ((rows[0] + rows[1]) + (rows[2] + rows[3])) + (rows[4] + rows[5])
        mean = jnp.sum(tot, axis=-1, keepdims=True) * (1.0 / D)
        cs = [r - mean for r in rows]
        sq = [c * c for c in cs]
        sq = ((sq[0] + sq[1]) + (sq[2] + sq[3])) + (sq[4] + sq[5])
        inv = lax.rsqrt(jnp.sum(sq, axis=-1, keepdims=True) * (1.0 / D) + NORM_EPS) * INV_SQRT2
        for l in range(LB):
            sn_ref[pl.ds(pl.multiple_of(n * 64, 64), 64), l * 128:(l + 1) * 128] = (cs[l] * inv).astype(jnp.bfloat16)
        return 0
    lax.fori_loop(0, 8, some_rows, 0, unroll=8)


def hidden_chunk(c, sn_ref, w1_ref, ph_ref, g):
    h = jnp.dot(sn_ref[...], w1_ref[c], preferred_element_type=jnp.float32)
    h = h + h * lax.erf(h)
    ph_ref[c, g * GROUP:(g + 1) * GROUP, :] = jnp.sum(h.reshape(64, GROUP, HC), axis=0)


def encode(groups, more_loads, x_hbm, down_hbm, taps_ref, w1_hbm, w2_hbm, ls_ref, emb_ref,
                  x_ref, down_ref, w1_ref, w2_ref, s_ref, l0_ref, l1_ref, r0_ref, r1_ref, sp_ref, sn_ref, tap_ref, x_tmp, y_tmp, ph_ref, pr_ref, sems):
    l_bufs, r_bufs = (l0_ref, l1_ref), (r0_ref, r1_ref)
    x_copy = [pltpu.make_async_copy(x_hbm.at[pl.ds(g * GROUP, GROUP)], x_ref.at[pl.ds(g * GROUP, GROUP)], sems.at[g])
              for g in range(groups)]
    down_copy = pltpu.make_async_copy(down_hbm, down_ref, sems.at[groups])
    w1_copy = [pltpu.make_async_copy(w1_hbm.at[:, pl.ds(c * HC, HC)], w1_ref.at[c], sems.at[groups + 2 + c]) for c in range(LB)]
    w2_copy = pltpu.make_async_copy(w2_hbm, w2_ref, sems.at[groups + 1])
    x_copy[0].start()
    down_copy.start()
    fill_taps(taps_ref, tap_ref)
    x_copy[0].wait()
    x_copy[1].start()
    for copy in w1_copy:
        copy.start()
    def only_norm(n, _):
        norm_rows(n, x_ref, s_ref, 0)
        return 0
    lax.fori_loop(0, GROUP * 4, only_norm, 0, unroll=8)
    make_patches(s_ref, l0_ref)
    for g in range(2, groups):
        x_copy[g].start()
    w2_copy.start()
    for copy in more_loads:
        copy.start()
    down_copy.wait()

    def norm_and_reduce(g_norm, g_red):
        per = GROUP * 4 // BSPLIT

        def step(n, _):
            if g_norm < groups:
                for k in range(per):
                    norm_rows(n * per + k, x_ref, s_ref, g_norm)
            if g_red < groups:
                reduce_rows(n, l_bufs[g_red % 2], down_ref, r_bufs[g_red % 2])
            return 0
        if g_norm < groups:
            x_copy[g_norm].wait()
        lax.fori_loop(0, BSPLIT, step, 0)
        if g_norm < groups:
            make_patches(s_ref, l_bufs[g_norm % 2])
    norm_and_reduce(1, 0)

    for g in range(groups + 1):
        if g == 1:
            for copy in w1_copy:
                copy.wait()

        def step(n, _):
            if g < groups:
                conv_lane(n, r_bufs[g % 2], tap_ref, sp_ref, pr_ref, x_tmp, y_tmp, g)
            if g >= 1:
                hidden_chunk(n, sn_ref, w1_ref, ph_ref, g - 1)
            return 0
        lax.fori_loop(0, LB, step, 0, unroll=3 if g == groups else 1)
        if g < groups:
            norm_spatial(sp_ref, sn_ref)
        if g + 1 < groups:
            norm_and_reduce(g + 2, g + 1)

    w2_copy.wait()
    br = jnp.dot(jnp.concatenate(split_bf16(jnp.concatenate([ph_ref[c] for c in range(LB)], axis=-1)), axis=0), w2_ref[...], preferred_element_type=jnp.float32)
    nt = groups * GROUP
    br = br[:nt] + br[nt:]
    pr = jnp.concatenate([pr_ref[l] for l in range(LB)], axis=-1)
    pooled = (pr + ls_ref[...].reshape(1, D) * (INV_SQRT2 * br)) * (1.0 / (HALF * HALF))
    c = pooled - jnp.mean(pooled, axis=-1, keepdims=True)
    v = jnp.mean(c * c, axis=-1, keepdims=True)
    emb_ref[...] = (c * lax.rsqrt(v + NORM_EPS)).astype(jnp.bfloat16)


HEADS = 12
HEAD_DIM = 64
SEQ_DEV = 192
HALF_SEQ = 96
CAP = 2
CODED = D + 128
FAR_NEGATIVE = -1e30
MESH = pl.DeviceIdType.MESH


def row_norm(values):
    center = values - jnp.sum(values, axis=-1, keepdims=True) * (1.0 / D)
    spread = jnp.sum(center * center, axis=-1, keepdims=True) * (1.0 / D)
    return center * lax.rsqrt(spread + NORM_EPS)


def greet(slides, ctxs):
    count = slides * ctxs
    me = lax.axis_index("slide") * ctxs + lax.axis_index("ctx")
    barrier = pltpu.get_barrier_semaphore()

    def one(k, _):
        peer = lax.rem(me + k, count)
        pl.semaphore_signal(barrier, inc=1, device_id=(peer // ctxs, lax.rem(peer, ctxs)), device_id_type=MESH)
        return 0
    lax.fori_loop(1, count, one, 0)


def slide_layer(slides, ctxs, loads, emb_ref, slide_ref, pos_ref, len_ref, out_ref,
                wqkv_ref, wout_ref, send_ref, recv_ref, rows_ref, k_ref, v_ref, q_ref, att_ref,
                a2a_send, a2a_recv, own_sem, ring_send, ring_recv):
    load_qkv, load_out = loads
    count = slides * ctxs
    tiles = emb_ref.shape[0]
    total = ctxs * SEQ_DEV
    slide = lax.axis_index("slide")
    ctx = lax.axis_index("ctx")
    me = slide * ctxs + ctx
    pos = pos_ref[...].reshape(1, tiles).astype(jnp.float32)
    block = jnp.floor((pos + 0.5) * (1.0 / SEQ_DEV))
    owner = slide_ref[...].reshape(1, tiles).astype(jnp.float32) * ctxs + block
    code = pos - block * SEQ_DEV + 1.0
    line = lax.broadcasted_iota(jnp.int32, (count * CAP, tiles), 0)
    target = (line // CAP).astype(jnp.float32)
    member = jnp.where(owner == target, 1.0, 0.0)
    before = lax.broadcasted_iota(jnp.int32, (tiles, tiles), 0) < lax.broadcasted_iota(jnp.int32, (tiles, tiles), 1)
    rank = jnp.dot(member.astype(jnp.bfloat16), jnp.where(before, 1.0, 0.0).astype(jnp.bfloat16),
                   preferred_element_type=jnp.float32)
    chosen = jnp.where(rank == (line % CAP).astype(jnp.float32), member, 0.0)
    codes = jnp.broadcast_to(jnp.sum(chosen * code, axis=1, keepdims=True), (count * CAP, 128))
    moved = jnp.dot(chosen.astype(jnp.bfloat16), emb_ref[...], preferred_element_type=jnp.float32)
    send_ref[:, :, :D] = moved.reshape(count, CAP, D).astype(jnp.bfloat16)
    send_ref[:, :, D:] = codes.reshape(count, CAP, 128).astype(jnp.bfloat16)
    pl.semaphore_wait(pltpu.get_barrier_semaphore(), count - 1)

    own = pltpu.make_async_copy(send_ref.at[me], recv_ref.at[me], own_sem)
    own.start()

    def send(k, _):
        peer = lax.rem(me + k, count)
        pltpu.make_async_remote_copy(
            src_ref=send_ref.at[peer], dst_ref=recv_ref.at[me], send_sem=a2a_send, recv_sem=a2a_recv,
            device_id=(peer // ctxs, lax.rem(peer, ctxs)), device_id_type=MESH).start()
        return 0
    lax.fori_loop(1, count, send, 0)
    own.wait()
    rest = pl.ds(0, count - 1)
    whole = pltpu.make_async_remote_copy(
        src_ref=send_ref.at[rest], dst_ref=recv_ref.at[rest], send_sem=a2a_send, recv_sem=a2a_recv,
        device_id=(slide, ctx), device_id_type=MESH)
    whole.wait_recv()

    arrived = recv_ref[...].reshape(count * CAP, CODED)
    got = arrived[:, D:].astype(jnp.float32)
    lane = lax.broadcasted_iota(jnp.int32, (count * CAP, 128), 1).astype(jnp.float32) + 1.0
    pick = jnp.concatenate([jnp.where(got == lane, 1.0, 0.0), jnp.where(got == lane + 128.0, 1.0, 0.0)], axis=1)
    mine = lax.dot_general(pick.astype(jnp.bfloat16), arrived[:, :D], (((0,), (0,)), ((), ())),
                           preferred_element_type=jnp.float32)
    rows_ref[ctx] = mine[:SEQ_DEV].astype(jnp.bfloat16)

    right = lax.rem(ctx + 1, ctxs)
    left = lax.rem(ctx + ctxs - 1, ctxs)
    far = lax.rem(ctx + 2, ctxs)
    first, second = pl.ds(0, HALF_SEQ), pl.ds(HALF_SEQ, HALF_SEQ)

    def hop(n, blk, half, to):
        return pltpu.make_async_remote_copy(
            src_ref=rows_ref.at[blk, half], dst_ref=rows_ref.at[blk, half],
            send_sem=ring_send.at[n], recv_sem=ring_recv.at[n], device_id=(slide, to), device_id_type=MESH)

    def keys_values(blk):
        ln = row_norm(rows_ref[blk].astype(jnp.float32)).astype(jnp.bfloat16)
        at = pl.ds(pl.multiple_of(blk * SEQ_DEV, 64), SEQ_DEV)
        k_ref[at, :] = jnp.dot(ln, wqkv_ref[:, D:2 * D], preferred_element_type=jnp.float32).astype(jnp.bfloat16)
        v_ref[at, :] = jnp.dot(ln, wqkv_ref[:, 2 * D:], preferred_element_type=jnp.float32).astype(jnp.bfloat16)
        return ln
    own_hops = [hop(0, ctx, first, right), hop(1, ctx, second, left), hop(2, ctx, second, right), hop(3, ctx, first, left)]
    for h in own_hops:
        h.start()
    load_qkv.wait()
    ln = keys_values(ctx)
    q = jnp.dot(ln, wqkv_ref[:, :D], preferred_element_type=jnp.float32)
    q_ref[...] = (q.astype(jnp.bfloat16).astype(jnp.float32) * HEAD_DIM ** (-0.5)).astype(jnp.bfloat16)
    own_hops[0].wait_recv()
    onward = hop(4, left, first, right)
    onward.start()
    own_hops[1].wait_recv()
    back = hop(5, right, second, left)
    back.start()
    own_hops[2].wait_recv()
    own_hops[3].wait_recv()

    def near(n, _):
        keys_values(lax.rem(ctx + 1 + 2 * n, ctxs))
        return 0
    lax.fori_loop(0, 2, near, 0)
    onward.wait_recv()
    back.wait_recv()
    keys_values(far)
    for h in own_hops + [onward, back]:
        h.wait_send()
    whole.wait_send()
    load_out.wait()

    length = len_ref[slide]
    key = lax.broadcasted_iota(jnp.int32, (1, total), 1)
    bias = jnp.where(key < length, 0.0, FAR_NEGATIVE)
    low = lax.broadcasted_iota(jnp.int32, (SEQ_DEV, 128), 1) < HEAD_DIM
    for pair in range(HEADS // 2):
        cols = slice(pair * 128, pair * 128 + 128)
        q2 = q_ref[:, cols]
        zero = jnp.zeros_like(q2)
        both = jnp.concatenate([jnp.where(low, q2, zero), jnp.where(low, zero, q2)], axis=0)
        s = lax.dot_general(both, k_ref[:, cols], (((1,), (1,)), ((), ())), preferred_element_type=jnp.float32) + bias
        w = jnp.exp(s - jnp.max(s, axis=-1, keepdims=True))
        ext = jnp.concatenate([v_ref[:, cols], jnp.full((total, 128), 1.0, jnp.bfloat16)], axis=1)
        o = jnp.dot(w.astype(jnp.bfloat16), ext, preferred_element_type=jnp.float32)
        o = o[:, :128] * (1.0 / o[:, 128:])
        att_ref[:, cols] = jnp.where(low, o[:SEQ_DEV], o[SEQ_DEV:]).astype(jnp.bfloat16)
    out = jnp.dot(att_ref[...], wout_ref[...], preferred_element_type=jnp.float32)
    out = out + rows_ref[ctx].astype(jnp.float32)
    row = lax.broadcasted_iota(jnp.int32, (SEQ_DEV, 1), 0) + ctx * SEQ_DEV
    out_ref[...] = jnp.where(row < length, out, 0.0).astype(jnp.bfloat16)


def whole_kernel(groups, slides, ctxs, x_hbm, down_hbm, taps_ref, w1_hbm, w2_hbm, ls_ref, wqkv_hbm, wout_hbm,
                 slide_ref, pos_ref, len_ref, out_ref, emb_ref, load_sem, wqkv_ref, wout_ref, send_ref, recv_ref, rows_ref,
                 k_ref, v_ref, q_ref, att_ref, a2a_send, a2a_recv, own_sem, ring_send, ring_recv, *encoder_refs):
    greet(slides, ctxs)
    loads = (pltpu.make_async_copy(wqkv_hbm, wqkv_ref, load_sem.at[0]), pltpu.make_async_copy(wout_hbm, wout_ref, load_sem.at[1]))
    encode(groups, loads, x_hbm, down_hbm, taps_ref, w1_hbm, w2_hbm, ls_ref, emb_ref, *encoder_refs)
    slide_layer(slides, ctxs, loads, emb_ref, slide_ref, pos_ref, len_ref, out_ref,
                wqkv_ref, wout_ref, send_ref, recv_ref, rows_ref, k_ref, v_ref, q_ref, att_ref,
                a2a_send, a2a_recv, own_sem, ring_send, ring_recv)


def shards(x, down, taps, w1, w2, ls, qkv_weight, out_weight, tile_slide, tile_pos, slide_len):
    slides, ctxs = lax.axis_size("slide"), lax.axis_size("ctx")
    nt = x.shape[0]
    groups = nt // GROUP
    count = slides * ctxs
    total = ctxs * SEQ_DEV
    hbm = pl.BlockSpec(memory_space=pl.ANY)
    vmem = pl.BlockSpec(memory_space=pltpu.VMEM)
    return pl.pallas_call(
        functools.partial(whole_kernel, groups, slides, ctxs),
        out_shape=jax.ShapeDtypeStruct((SEQ_DEV, D), jnp.bfloat16),
        in_specs=[hbm, hbm, vmem, hbm, hbm, vmem, hbm, hbm, vmem, vmem, pl.BlockSpec(memory_space=pltpu.SMEM)],
        out_specs=vmem,
        scratch_shapes=[
            pltpu.VMEM((nt, D), jnp.bfloat16), pltpu.SemaphoreType.DMA((2,)),
            pltpu.VMEM((D, 3 * D), jnp.bfloat16), pltpu.VMEM((D, D), jnp.bfloat16),
            pltpu.VMEM((count, CAP, CODED), jnp.bfloat16), pltpu.VMEM((count, CAP, CODED), jnp.bfloat16),
            pltpu.VMEM((ctxs, SEQ_DEV, D), jnp.bfloat16),
            pltpu.VMEM((total, D), jnp.bfloat16), pltpu.VMEM((total, D), jnp.bfloat16),
            pltpu.VMEM((SEQ_DEV, D), jnp.bfloat16), pltpu.VMEM((SEQ_DEV, D), jnp.bfloat16),
            pltpu.SemaphoreType.DMA, pltpu.SemaphoreType.DMA, pltpu.SemaphoreType.DMA,
            pltpu.SemaphoreType.DMA((6,)), pltpu.SemaphoreType.DMA((6,)),
            pltpu.VMEM((nt, 16, 16, C_IN), jnp.bfloat16),
            pltpu.VMEM((4 * C_IN, D), jnp.bfloat16),
            pltpu.VMEM((LB, D, HC), jnp.bfloat16),
            pltpu.VMEM((MLP, D), jnp.bfloat16),
            pltpu.VMEM((3, GROUP * PITCH, 128), jnp.float32),
            pltpu.VMEM((64 * GROUP, 4 * C_IN), jnp.bfloat16),
            pltpu.VMEM((64 * GROUP, 4 * C_IN), jnp.bfloat16),
            pltpu.VMEM((LB, 64, GROUP, 128), jnp.float32),
            pltpu.VMEM((LB, 64, GROUP, 128), jnp.float32),
            pltpu.VMEM((LB, 64, GROUP, 128), jnp.float32),
            pltpu.VMEM((64 * GROUP, D), jnp.bfloat16),
            pltpu.VMEM((LB, len(TAP_SUMS), 8, 128), jnp.float32),
            pltpu.VMEM((12, 3, 4, GROUP, 128), jnp.float32),
            pltpu.VMEM((13, HALF, GROUP, 128), jnp.float32),
            pltpu.VMEM((LB, nt, HC), jnp.float32),
            pltpu.VMEM((LB, nt, 128), jnp.float32),
            pltpu.SemaphoreType.DMA((groups + 2 + LB,)),
        ],
        compiler_params=pltpu.CompilerParams(collective_id=0, has_side_effects=True, vmem_limit_bytes=60 << 20),
        name="whole",
    )(x, down, taps, w1, w2, ls, qkv_weight[0], out_weight[0], tile_slide, tile_pos, slide_len)


def solution(mesh):
    whole = P(("slide", "ctx"))
    return jax.shard_map(
        shards,
        mesh=mesh,
        in_specs=(whole, P(), P(), P(), P(), P(), P(), P(), whole, whole, P()),
        out_specs=whole,
        check_vma=False,
    )
```
